256 devices in a mesh: sky: 8 (over z), chan: 32 (over x, y, core).
Axes of the slice: x: 4, y: 4, z: 8, core: 2. Of those that a mesh axis runs over, the one named last changes fastest.
Arguments:
- beam_images: float32 [32, 2, 288, 16384], P('sky', None, 'chan'), may hold values from -6 to 6
- beam_weights: float32 [32, 16384], P('sky'), may hold values from 0.05 to 1
- offsets: int32 [32], P('sky'), may hold values from 0 to 131071, as said below
Outputs:
- beam_residuals: float32 [32, 2, 288, 16384], P('sky', None, 'chan')
- depth_model: float32 [2, 512, 131072], P(None, None, ('sky', 'chan'))
The draws below stay inside these ranges and needn't reach their ends.
Inputs may be any that keep to these rules, and one draw needn't show every extreme that they name: `offsets`: beam b starts in tile b // 4: its offset lies in [(b // 4) * 16384, (b // 4 + 1) * 16384).
All inputs are finite; a program needn't handle non-finite values.
Results may differ from the reference program's by a relative error of at most 0.00045.
Values sent between devices are 32-bit elements; how exact they have to be, the bound alone decides.
A program may use at most 128 MiB of HBM per device.

```python
import math
import jax
import jax.numpy as jnp
from jax import lax

C = 288
F = 512
PIX_SKY = 16384
BEAMS_DEV = 4
ITERS = 3
BEAMS = 32
NPIX = 131072


def draw_offsets(key, part):
    tiles = jnp.arange(BEAMS, dtype=jnp.int32) // BEAMS_DEV * PIX_SKY
    return tiles + jax.random.randint(jax.random.fold_in(key, 17), (BEAMS,), 0, PIX_SKY, dtype=jnp.int32)


def level_of(key, shape, pieces, low, largest):
    level, own = 1.0, jax.random.fold_in(key, 6)
    for position, parts in pieces:
        draws = jnp.exp(jax.random.uniform(jax.random.fold_in(own, position), (parts,), jnp.float32, low / len(pieces), largest / len(pieces)))
        level = level * jnp.repeat(draws, shape[position] // parts).reshape([-1 if axis == position else 1 for axis in range(len(shape))])
    return level


def gaussian(own_key, extent, width, bound, pieces=(), kind=jnp.bfloat16):
    factor_of = level_of(own_key, extent, pieces, -0.22, 0.18) if pieces else 1.0
    array = jax.random.normal(own_key, extent, jnp.float32) * width * factor_of
    return jnp.minimum(jnp.maximum(array, -bound), bound).astype(kind)


def setup_inputs(seed: int = 0) -> dict:
    arg_keys = jax.random.split(jax.random.key(seed), 4)
    beam_images = gaussian(arg_keys[0], (BEAMS, 2, C, PIX_SKY), 1.0, 6.0, ((0, 8), (2, 32)), jnp.float32)
    beam_weights = jnp.clip(jnp.exp(math.log(1.0) - 2.9957323 * jax.random.uniform(arg_keys[1], (BEAMS, PIX_SKY), jnp.float32) ** level_of(arg_keys[1], (BEAMS, PIX_SKY), ((0, 8),), -0.2, 0.2)), 0.05, 1.0)
    offsets = draw_offsets(jax.random.fold_in(arg_keys[3], 71), 0)
    return {"beam_images": beam_images, "beam_weights": beam_weights, "offsets": offsets}


BAND_LOW = 800000000.0
BAND_WIDTH = 288000000.0
LIGHT = 299792458.0
DEPTH_STEP = 20.0
COMBINE_FLOOR = 0.5
THRESH_FRAC = 0.25
THRESH_BASE = 0.005
STEP_GAIN = 0.5

def depth_tables():
    channel = jnp.arange(C, dtype=jnp.float32)
    freq = BAND_LOW + (channel + 0.5) * (BAND_WIDTH / C)
    lam_sq = (LIGHT / freq) ** 2
    lam_sq = lam_sq - jnp.mean(lam_sq)
    depth = (jnp.arange(F, dtype=jnp.float32) - F // 2) * DEPTH_STEP
    angle = 2.0 * depth[:, None] * lam_sq[None, :]
    cosine = jnp.cos(angle)
    sine = jnp.sin(angle)
    synth = jnp.concatenate([jnp.concatenate([cosine, sine], 1), jnp.concatenate([-sine, cosine], 1)], 0) / C
    forward = jnp.concatenate([jnp.concatenate([cosine.T, -sine.T], 1), jnp.concatenate([sine.T, cosine.T], 1)], 0)
    return (synth, forward)

def matmul(left, right):
    return jnp.dot(left, right, preferred_element_type=jnp.float32, precision=lax.Precision.HIGHEST)

def magnitude(field):
    return jnp.sqrt(field[:F] ** 2 + field[F:] ** 2)

def shrink(field, thresh):
    mag = magnitude(field)
    factor = jnp.maximum(mag - thresh, 0.0) / jnp.maximum(mag, thresh)
    return field * jnp.concatenate([factor, factor], 0)

def deconvolve(combined, synth, forward):
    dirty = matmul(synth, combined)
    thresh = THRESH_FRAC * lax.optimization_barrier(jnp.max(magnitude(dirty), axis=0, keepdims=True)) + THRESH_BASE
    model = jnp.zeros(dirty.shape, jnp.float32)
    for step in range(ITERS):
        resid = combined - matmul(forward, model)
        model = shrink(model + STEP_GAIN * matmul(synth, resid), thresh)
    resid = combined - matmul(forward, model)
    return (model, resid)

def reference(beam_images, beam_weights, offsets):
    total = NPIX + PIX_SKY
    numer = jnp.zeros((2, C, total), jnp.float32)
    wsum = jnp.zeros((total,), jnp.float32)

    def add_beam(index, carry):
        numer, wsum = carry
        start = offsets[index].astype(jnp.int32)
        weight = beam_weights[index]
        old = lax.dynamic_slice_in_dim(numer, start, PIX_SKY, 2)
        numer = lax.dynamic_update_slice_in_dim(numer, old + weight * beam_images[index], start, 2)
        oldw = lax.dynamic_slice_in_dim(wsum, start, PIX_SKY, 0)
        wsum = lax.dynamic_update_slice_in_dim(wsum, oldw + weight, start, 0)
        return (numer, wsum)
    numer, wsum = lax.fori_loop(0, BEAMS, add_beam, (numer, wsum))
    combined = numer[:, :, :NPIX] / (wsum[:NPIX] + COMBINE_FLOOR)
    synth, forward = depth_tables()
    model, resid = deconvolve(combined.reshape(2 * C, NPIX), synth, forward)
    padded = jnp.concatenate([resid.reshape(2, C, NPIX), jnp.zeros((2, C, PIX_SKY), jnp.float32)], 2)

    def read_beam(pair):
        weight, start = pair
        return weight * lax.dynamic_slice_in_dim(padded, start.astype(jnp.int32), PIX_SKY, 2)
    beam_residuals = lax.map(read_beam, (beam_weights, offsets))
    return (beam_residuals, model.reshape(2, F, NPIX))
```

```python
import functools

import jax
import jax.numpy as jnp
import ml_dtypes
import numpy as np
from jax import lax
from jax.experimental import pallas as pl
from jax.experimental.pallas import tpu as pltpu
from jax.sharding import PartitionSpec as P

C = 288
F = 512
H = F // 2
BEAMS_DEV = 4
ITERS = 3
SKY = 8
CHAN = 32
PER = C // CHAN
MAIN = CHAN * 8
CHUNKS = 4

BAND_LOW = 800000000.0
BAND_WIDTH = 288000000.0
LIGHT = 299792458.0
DEPTH_STEP = 20.0
COMBINE_FLOOR = 0.5
THRESH_FRAC = 0.25
THRESH_BASE = 0.005
STEP_GAIN = 0.5
MESH = pl.DeviceIdType.MESH
F32 = jnp.float32
BF16 = jnp.bfloat16
VMEM_LIMIT = 56 << 20


def tables():
    one = np.float32
    channel = np.arange(C, dtype=one)
    freq = one(BAND_LOW) + (channel + one(0.5)) * one(BAND_WIDTH / C)
    lam = one(LIGHT) / freq
    lam_sq = lam * lam
    lam_sq = lam_sq - np.mean(lam_sq, dtype=one)
    depth = (H - np.arange(H, dtype=one)) * one(DEPTH_STEP)
    angle = (one(2.0) * depth)[:, None] * lam_sq[None, :]
    order = np.arange(C).reshape(CHAN, PER)
    order = np.concatenate([order[:, :8].reshape(-1), order[:, 8]])
    angle = angle[:, order].astype(np.float64)
    cosine, sine = np.cos(angle).astype(one), np.sin(angle).astype(one)

    def parts(value):
        high = value.astype(ml_dtypes.bfloat16)
        return high, (value - high.astype(one)).astype(ml_dtypes.bfloat16)

    extra = np.zeros((8, C), one)
    extra[0] = 1.0
    synth = np.concatenate([cosine, sine, extra], 0) / one(C)
    high, low = parts(synth)
    synth = np.concatenate([high[:, :MAIN], high[:, :MAIN], low[:, :MAIN], high[:, MAIN:], high[:, MAIN:], low[:, MAIN:]], 1)
    high, low = parts(np.concatenate([cosine.T, sine.T], 1))
    forward = np.concatenate([high, high, low], 1)
    turn = np.zeros((H, H), one)
    turn[np.arange(H), (-np.arange(H)) % H] = 1.0
    turn = np.concatenate([turn] * 3, 1).astype(ml_dtypes.bfloat16)
    return synth, forward, turn


def split(value):
    high = value.astype(BF16)
    return high, (value - high.astype(F32)).astype(BF16)


def dot(left, right):
    return jnp.dot(left, right, preferred_element_type=F32)


def sub_iota():
    return lax.broadcasted_iota(jnp.int32, (8, 128), 0)


def lane_iota():
    return lax.broadcasted_iota(jnp.int32, (8, 128), 1)


def swap_pairs(tiles):
    rows = sub_iota()
    low, even = rows < 4, (rows & 2) == 0
    a0, a1, a2, a3 = tiles
    b0 = jnp.where(low, a0, pltpu.roll(a2, 4, 0))
    b1 = jnp.where(low, a1, pltpu.roll(a3, 4, 0))
    b2 = jnp.where(low, pltpu.roll(a0, 4, 0), a2)
    b3 = jnp.where(low, pltpu.roll(a1, 4, 0), a3)
    return (
        jnp.where(even, b0, pltpu.roll(b1, 2, 0)),
        jnp.where(even, pltpu.roll(b0, 6, 0), b1),
        jnp.where(even, b2, pltpu.roll(b3, 2, 0)),
        jnp.where(even, pltpu.roll(b2, 6, 0), b3),
    )


def pair_rows(rows8, first):
    rows = sub_iota()
    row = [jnp.broadcast_to(rows8[first + k : first + k + 1], (8, 128)) for k in range(4)]
    return jnp.where(rows < 4, jnp.where(rows < 2, row[0], row[1]), jnp.where(rows < 6, row[2], row[3]))


def combine_kernel(start_ref, x_ref, x9_ref, w_ref, o_ref, o9_ref, ow_ref):
    beam = pl.program_id(0)

    @pl.when(beam == 0)
    def _():
        o_ref[...] = jnp.zeros_like(o_ref)
        o9_ref[...] = jnp.zeros_like(o9_ref)
        ow_ref[...] = jnp.zeros_like(ow_ref)

    start = start_ref[beam]
    whole, shift = start // 128, start % 128
    tile, part = whole // 4, (whole % 4) * 2
    lanes, rows = lane_iota(), sub_iota()
    stays = lanes >= shift
    below = rows >= part
    zero = jnp.zeros((8, 128), F32)

    def add_narrow(at, value, last_shift, last_turn, ref):
        rolled = pltpu.roll(value, shift, 1)
        moved = pltpu.roll(rolled, 2, 0)
        joined = jnp.where(stays, rolled, jnp.where(rows >= 2, moved, last_shift))
        turned = pltpu.roll(joined, part, 0)
        ref[at] += jnp.where(below, turned, last_turn)
        return moved, turned

    def step(i, carry):
        last, narrow9, narrow_w = carry
        weights = w_ref[0, pl.ds(pl.multiple_of(i * 8, 8), 8), :]
        for half in range(2):
            at = i * 2 + half
            row = pl.ds(pl.multiple_of(at * 8, 8), 8)
            pair = pair_rows(weights, half * 4)
            narrow9 = add_narrow(tile + at, x9_ref[0, 0, row, :] * pair, *narrow9, o9_ref)
            narrow_w = add_narrow(tile + at, pair, *narrow_w, ow_ref)
            blocks = [swap_pairs([x_ref[0, 4 * g + k, row, :] for k in range(4)]) for g in range(2)]
            for k in range(4):
                weight = jnp.broadcast_to(weights[half * 4 + k : half * 4 + k + 1], (8, 128))
                rolled = [pltpu.roll(blocks[g][k] * weight, shift, 1) for g in range(2)]
                for g in range(2):
                    o_ref[whole + at * 4 + k, 8 * g : 8 * g + 8] += jnp.where(stays, rolled[g], last[g])
                last = rolled
        return last, narrow9, narrow_w

    last, narrow9, narrow_w = lax.fori_loop(0, 16, step, ([zero, zero], (zero, zero), (zero, zero)))
    for g in range(2):
        o_ref[whole + 128, 8 * g : 8 * g + 8] += jnp.where(stays, 0.0, last[g])
    add_narrow(tile + 32, zero, *narrow9, o9_ref)
    add_narrow(tile + 32, zero, *narrow_w, ow_ref)


def gather_kernel(start_ref, r_ref, r9_ref, w_ref, o_ref):
    beam = pl.program_id(0)
    start = start_ref[beam]
    end = start_ref[BEAMS_DEV]
    whole, shift = start // 128, start % 128
    tile, part = whole // 4, (whole % 4) * 2
    lanes, rows = lane_iota(), sub_iota()
    stays = lanes < 128 - shift
    above = rows < 8 - part
    back = (128 - shift) % 128
    turn = (8 - part) % 8

    def block(at, g):
        value = r_ref[at, 8 * g : 8 * g + 8]
        return pltpu.roll(jnp.where(at < end, value, 0.0), back, 1)

    def turned9(at):
        return pltpu.roll(jnp.where(at * 4 < end, r9_ref[at], 0.0), turn, 0)

    def rolled9(first, second):
        return pltpu.roll(jnp.where(above, first, second), back, 1)

    first = turned9(tile)
    second = turned9(tile + 1)

    def step(i, carry):
        now, rolled, turned = carry
        weights = w_ref[0, pl.ds(pl.multiple_of(i * 8, 8), 8), :]
        for half in range(2):
            at = i * 2 + half
            row = pl.ds(pl.multiple_of(at * 8, 8), 8)
            beyond = turned9(jnp.minimum(tile + at + 2, 63))
            after = rolled9(turned, beyond)
            moved = jnp.where(rows < 6, pltpu.roll(rolled, 6, 0), pltpu.roll(after, 6, 0))
            o_ref[0, 8, row, :] = jnp.where(stays, rolled, moved) * pair_rows(weights, half * 4)
            rolled, turned = after, beyond
            results = [[], []]
            for k in range(4):
                weight = jnp.broadcast_to(weights[half * 4 + k : half * 4 + k + 1], (8, 128))
                later = [block(whole + at * 4 + k + 1, g) for g in range(2)]
                for g in range(2):
                    results[g].append(jnp.where(stays, now[g], later[g]) * weight)
                now = later
            for g in range(2):
                for k, value in enumerate(swap_pairs(results[g])):
                    o_ref[0, 4 * g + k, row, :] = value
        return now, rolled, turned

    lax.fori_loop(0, 16, step, ([block(whole, g) for g in range(2)], rolled9(first, second), second))


def exchange_kernel(
    num, num9, wsum, synth, forward, turn, res, res9, depth,
    hx, hx9, hw, sb, sb9, rx, rx9, bk, bk9, flat, rhs_c, rhs_f, model_re, model_im,
    up_send, up_recv, up9_send, up9_recv, upw_send, upw_recv,
    to_send, to_recv, to9_send, to9_recv,
    back_send, back_recv, back9_send, back9_recv,
    down_send, down_recv, down9_send, down9_recv,
):
    sky, me = lax.axis_index("sky"), lax.axis_index("chan")
    up, down = lax.rem(sky + 1, SKY), lax.rem(sky + SKY - 1, SKY)
    mine = pl.ds(pl.multiple_of(me * 8, 8), 8)

    barrier = pltpu.get_barrier_semaphore()

    def greet(d, carry):
        pl.semaphore_signal(barrier, inc=1, device_id=(sky, lax.rem(me + d, CHAN)), device_id_type=MESH)
        return carry

    lax.fori_loop(1, CHAN, greet, 0)
    for other in (up, down):
        pl.semaphore_signal(barrier, inc=1, device_id=(other, me), device_id_type=MESH)
    pl.semaphore_wait(barrier, CHAN + 1)

    def remote(src, dst, send, recv, device):
        return pltpu.make_async_remote_copy(
            src_ref=src, dst_ref=dst, send_sem=send, recv_sem=recv, device_id=device, device_id_type=MESH
        )

    second = pl.ds(CHAN, CHAN)
    first = pl.ds(0, CHAN)
    up_w = remote(wsum.at[CHAN + me], hw, upw_send, upw_recv, (up, me))
    up_9 = remote(num9.at[second], hx9, up9_send, up9_recv, (up, me))

    def up_copy(s):
        return remote(num.at[second, s], hx.at[:, s], up_send.at[s], up_recv.at[s], (up, me))

    def down_copy(s):
        return remote(res.at[first, s], res.at[second, s], down_send.at[s], down_recv.at[s], (down, me))

    down_9 = remote(res9.at[first], res9.at[second], down9_send, down9_recv, (down, me))

    up_copy(0).start()
    up_9.start()
    up_w.start()
    for s in range(1, CHUNKS):
        up_copy(s).start()

    def spread(s):
        up_copy(s).wait_recv()
        sb[s] = num[:CHAN, s] + jnp.where(sky > 0, hx[:, s], 0.0)
        pltpu.make_async_copy(sb.at[s, me], rx.at[s, me], to_recv.at[s]).start()

        def send(d, carry):
            to = lax.rem(me + d, CHAN)
            remote(sb.at[s, to], rx.at[s, me], to_send.at[s], to_recv.at[s], (sky, to)).start()
            return carry

        lax.fori_loop(1, CHAN, send, 0)

    def spread9():
        up_9.wait_recv()
        up_w.wait_recv()
        sb9[...] = num9[:CHAN] + jnp.where(sky > 0, hx9[...], 0.0)
        pltpu.make_async_copy(sb9.at[me], rx9.at[mine], to9_recv).start()

        def send(d, carry):
            to = lax.rem(me + d, CHAN)
            remote(sb9.at[to], rx9.at[mine], to9_send, to9_recv, (sky, to)).start()
            return carry

        lax.fori_loop(1, CHAN, send, 0)

    is_zero = lax.broadcasted_iota(jnp.int32, (H, 128), 0) == 0

    def synthesis(field):
        high, low = split(field)
        rhs_c[0:MAIN] = high[:MAIN]
        rhs_c[MAIN : 2 * MAIN] = low[:MAIN]
        rhs_c[2 * MAIN : 3 * MAIN] = high[:MAIN]
        rhs_c[3 * MAIN : 3 * MAIN + 32] = high[MAIN:]
        rhs_c[3 * MAIN + 32 : 3 * MAIN + 64] = low[MAIN:]
        rhs_c[3 * MAIN + 64 : 3 * MAIN + 96] = high[MAIN:]
        out = dot(synth[...], rhs_c[...])
        cos_q, cos_u = out[:H, :128], out[:H, 128:]
        sin_q, sin_u = out[H:F, :128], out[H:F, 128:]
        plus_re = jnp.where(is_zero, out[F : F + 1, :128], cos_q + sin_u)
        plus_im = jnp.where(is_zero, out[F : F + 1, 128:], cos_u - sin_q)
        return plus_re, plus_im, cos_q - sin_u, cos_u + sin_q

    def residual():
        plus_re, plus_im = model_re[:H], model_im[:H]
        minus_re, minus_im = model_re[H:], model_im[H:]
        zero_re, zero_im = plus_re[0:1], plus_im[0:1]
        plus_re = jnp.where(is_zero, 0.0, plus_re)
        plus_im = jnp.where(is_zero, 0.0, plus_im)

        def put(value, row, column):
            high, low = split(value)
            columns = slice(column, column + 128)
            rhs_f[row : row + H, columns] = high
            rhs_f[F + row : F + row + H, columns] = low
            rhs_f[2 * F + row : 2 * F + row + H, columns] = high

        put(plus_re + minus_re, 0, 0)
        put(plus_im + minus_im, 0, 128)
        put(minus_im - plus_im, H, 0)
        put(plus_re - minus_re, H, 128)
        seen = dot(forward[...], rhs_f[...])
        return flat[...] - (seen + jnp.concatenate([zero_re, zero_im], 1))

    def deconvolve(s):
        pltpu.make_async_copy(rx.at[s], rx.at[s], to_recv.at[s]).wait()
        scale = wsum[me] + jnp.where(sky > 0, hw[...], 0.0) + COMBINE_FLOOR
        rows = lax.broadcasted_iota(jnp.int32, (8, 128), 0)
        scale = 1.0 / jnp.sum(jnp.where(rows == 2 * s, scale, 0.0), axis=0, keepdims=True)
        for q in range(2):
            columns = slice(128 * q, 128 * q + 128)
            flat[:MAIN, columns] = rx[s, :, pl.ds(q, 8, stride=2), :].reshape(MAIN, 128) * scale
            flat[MAIN:, columns] = rx9[pl.ds(2 * s + q, CHAN, stride=8), :] * scale
        dirty = synthesis(flat[...])
        re = jnp.concatenate([dirty[0], dirty[2]], 0)
        im = jnp.concatenate([dirty[1], dirty[3]], 0)
        mag = jnp.sqrt(re * re + im * im)
        thresh = THRESH_FRAC * jnp.max(mag, axis=0, keepdims=True) + THRESH_BASE
        mag = STEP_GAIN * mag
        factor = STEP_GAIN * (jnp.maximum(mag - thresh, 0.0) / jnp.maximum(mag, thresh))
        model_re[...] = re * factor
        model_im[...] = im * factor

        def iteration(_, carry):
            grown = synthesis(residual())
            for plus in range(2):
                part = slice(H * plus, H * plus + H)
                re = model_re[part] + STEP_GAIN * grown[2 * plus]
                im = model_im[part] + STEP_GAIN * grown[2 * plus + 1]
                mag = jnp.sqrt(re * re + im * im)
                factor = jnp.maximum(mag - thresh, 0.0) / jnp.maximum(mag, thresh)
                model_re[part] = re * factor
                model_im[part] = im * factor
            return carry

        lax.fori_loop(0, ITERS - 1, iteration, 0)
        rest = residual()
        for q in range(2):
            columns = slice(128 * q, 128 * q + 128)
            bk[s, :, pl.ds(q, 8, stride=2), :] = rest[:MAIN, columns].reshape(CHAN, 8, 128)
            bk9[pl.ds(2 * s + q, CHAN, stride=8), :] = rest[MAIN:, columns]
        pltpu.make_async_copy(bk.at[s, me], res.at[me, s], back_recv.at[s]).start()

        def send(d, carry):
            to = lax.rem(me + d, CHAN)
            remote(bk.at[s, to], res.at[me, s], back_send.at[s], back_recv.at[s], (sky, to)).start()
            return carry

        lax.fori_loop(1, CHAN, send, 0)

        lanes = pl.ds(pl.multiple_of(s * 128, 128), 128)
        depth[0, 0:H, lanes] = model_re[H:]
        depth[1, 0:H, lanes] = model_im[H:]
        plus = jnp.concatenate([model_re[:H], model_im[:H]], 1)
        high = plus.astype(BF16)
        plus = plus - high.astype(F32)
        middle = plus.astype(BF16)
        low = (plus - middle.astype(F32)).astype(BF16)
        rhs_f[0:H] = high
        rhs_f[H : 2 * H] = middle
        rhs_f[2 * H : 3 * H] = low
        turned = dot(turn[...], rhs_f[0 : 3 * H])
        depth[0, H:, lanes] = turned[:, :128]
        depth[1, H:, lanes] = turned[:, 128:]

    def send_back9():
        pltpu.make_async_copy(bk9.at[mine], res9.at[me], back9_recv).start()

        def send(d, carry):
            to = lax.rem(me + d, CHAN)
            row = pl.ds(pl.multiple_of(to * 8, 8), 8)
            remote(bk9.at[row], res9.at[me], back9_send, back9_recv, (sky, to)).start()
            return carry

        lax.fori_loop(1, CHAN, send, 0)

    def step(i, carry):
        @pl.when(i < CHUNKS)
        def _():
            spread(i)

        @pl.when(i == 0)
        def _():
            spread9()

        @pl.when(i == 1)
        def _():
            pltpu.make_async_copy(rx9, rx9, to9_recv).wait()

        @pl.when((i >= 1) & (i <= CHUNKS))
        def _():
            deconvolve(i - 1)

        @pl.when(i == CHUNKS)
        def _():
            send_back9()

        @pl.when(i >= 2)
        def _():
            s = i - 2
            pltpu.make_async_copy(bk.at[s], bk.at[s], back_recv.at[s]).wait()
            down_copy(s).start()

        return carry

    lax.fori_loop(0, CHUNKS + 2, step, 0)
    pltpu.make_async_copy(hx9, hx9, back9_recv).wait()
    down_9.start()

    others = pl.ds(0, CHAN - 1)
    up_w.wait_send()
    up_9.wait_send()
    for s in range(CHUNKS):
        up_copy(s).wait_send()
        pltpu.make_async_copy(sb.at[s, others], sb.at[s, others], to_send.at[s]).wait()
        pltpu.make_async_copy(sb.at[s, others], sb.at[s, others], back_send.at[s]).wait()
    pltpu.make_async_copy(sb9.at[others], sb9.at[others], to9_send).wait()
    pltpu.make_async_copy(sb9.at[others], sb9.at[others], back9_send).wait()
    for s in range(CHUNKS):
        down_copy(s).wait()
    down_9.wait()


def body(beam_images, beam_weights, offsets):
    synth, forward, turn = tables()
    sky = lax.axis_index("sky")
    start = offsets - sky * (CHAN * F)
    end = jnp.where(sky == SKY - 1, CHAN * CHUNKS, 2 * CHAN * CHUNKS)
    start = jnp.concatenate([start, jnp.broadcast_to(end, (1,)).astype(jnp.int32)])
    images = beam_images.reshape(4, 2, PER, 128, 128).transpose(0, 2, 3, 1, 4).reshape(4, PER, 256, 128)
    weights = beam_weights.reshape(4, 128, 128)
    shape = jax.ShapeDtypeStruct

    num, num9, wsum = pl.pallas_call(
        combine_kernel,
        grid_spec=pltpu.PrefetchScalarGridSpec(
            num_scalar_prefetch=1,
            grid=(BEAMS_DEV,),
            in_specs=[
                pl.BlockSpec((1, 8, 256, 128), lambda b, _: (b, 0, 0, 0)),
                pl.BlockSpec((1, 1, 256, 128), lambda b, _: (b, 8, 0, 0)),
                pl.BlockSpec((1, 128, 128), lambda b, _: (b, 0, 0)),
            ],
            out_specs=[
                pl.BlockSpec((256, 16, 128), lambda b, _: (0, 0, 0)),
                pl.BlockSpec((64, 8, 128), lambda b, _: (0, 0, 0)),
                pl.BlockSpec((64, 8, 128), lambda b, _: (0, 0, 0)),
            ],
        ),
        out_shape=[shape((256, 16, 128), F32), shape((64, 8, 128), F32), shape((64, 8, 128), F32)],
        compiler_params=pltpu.CompilerParams(vmem_limit_bytes=VMEM_LIMIT),
    )(start, images, images, weights)

    dma = pltpu.SemaphoreType.DMA
    vmem = pltpu.VMEM
    whole = pl.BlockSpec(memory_space=vmem)
    res, res9, depth = pl.pallas_call(
        exchange_kernel,
        in_specs=[whole] * 6,
        out_specs=[whole] * 3,
        out_shape=[
            shape((2 * CHAN, CHUNKS, 16, 128), F32),
            shape((2 * CHAN, 8, 128), F32),
            shape((2, F, F), F32),
        ],
        scratch_shapes=[
            vmem((CHAN, CHUNKS, 16, 128), F32),
            vmem((CHAN, 8, 128), F32),
            vmem((8, 128), F32),
            vmem((CHUNKS, CHAN, 16, 128), F32),
            vmem((CHAN, 8, 128), F32),
            vmem((CHUNKS, CHAN, 16, 128), F32),
            vmem((CHAN * 8, 128), F32),
            vmem((CHUNKS, CHAN, 16, 128), F32),
            vmem((CHAN * 8, 128), F32),
            vmem((C, 256), F32),
            vmem((3 * C, 256), BF16),
            vmem((3 * F, 256), BF16),
            vmem((F, 128), F32),
            vmem((F, 128), F32),
            dma((CHUNKS,)), dma((CHUNKS,)), dma, dma, dma, dma,
            dma((CHUNKS,)), dma((CHUNKS,)), dma, dma,
            dma((CHUNKS,)), dma((CHUNKS,)), dma, dma,
            dma((CHUNKS,)), dma((CHUNKS,)), dma, dma,
        ],
        compiler_params=pltpu.CompilerParams(collective_id=0, has_side_effects=True, vmem_limit_bytes=VMEM_LIMIT),
    )(num.reshape(2 * CHAN, CHUNKS, 16, 128), num9, wsum, jnp.asarray(synth), jnp.asarray(forward), jnp.asarray(turn))

    out = pl.pallas_call(
        gather_kernel,
        grid_spec=pltpu.PrefetchScalarGridSpec(
            num_scalar_prefetch=1,
            grid=(BEAMS_DEV,),
            in_specs=[
                pl.BlockSpec((256, 16, 128), lambda b, _: (0, 0, 0)),
                pl.BlockSpec((64, 8, 128), lambda b, _: (0, 0, 0)),
                pl.BlockSpec((1, 128, 128), lambda b, _: (b, 0, 0)),
            ],
            out_specs=pl.BlockSpec((1, PER, 256, 128), lambda b, _: (b, 0, 0, 0)),
        ),
        out_shape=shape((BEAMS_DEV, PER, 256, 128), F32),
        compiler_params=pltpu.CompilerParams(vmem_limit_bytes=VMEM_LIMIT),
    )(start, res.reshape(256, 16, 128), res9, weights)
    out = out.reshape(4, PER, 128, 2, 128).transpose(0, 3, 1, 2, 4).reshape(4, 2, PER, 128 * 128)
    return out, depth


def solution(mesh):
    return jax.shard_map(
        body,
        mesh=mesh,
        in_specs=(P("sky", None, "chan", None), P("sky", None), P("sky")),
        out_specs=(P("sky", None, "chan", None), P(None, None, ("sky", "chan"))),
        check_vma=False,
    )
```

```python
import functools

import jax
import jax.numpy as jnp
import ml_dtypes
import numpy as np
from jax import lax
from jax.experimental import pallas as pl
from jax.experimental.pallas import tpu as pltpu
from jax.sharding import PartitionSpec as P

C = 288
F = 512
H = F // 2
BEAMS_DEV = 4
ITERS = 3
SKY = 8
CHAN = 32
PER = C // CHAN
MAIN = CHAN * 8
CHUNKS = 4

BAND_LOW = 800000000.0
BAND_WIDTH = 288000000.0
LIGHT = 299792458.0
DEPTH_STEP = 20.0
COMBINE_FLOOR = 0.5
THRESH_FRAC = 0.25
THRESH_BASE = 0.005
STEP_GAIN = 0.5
MESH = pl.DeviceIdType.MESH
F32 = jnp.float32
BF16 = jnp.bfloat16
VMEM_LIMIT = 56 << 20
UNROLL = 8
STRAIGHT_UP = ()
STRAIGHT_DOWN = (3,)


def tables():
    one = np.float32
    channel = np.arange(C, dtype=one)
    freq = one(BAND_LOW) + (channel + one(0.5)) * one(BAND_WIDTH / C)
    lam = one(LIGHT) / freq
    lam_sq = lam * lam
    lam_sq = lam_sq - np.mean(lam_sq, dtype=one)
    depth = (H - np.arange(H, dtype=one)) * one(DEPTH_STEP)
    angle = (one(2.0) * depth)[:, None] * lam_sq[None, :]
    order = np.arange(C).reshape(CHAN, PER)
    order = np.concatenate([order[:, :8].reshape(-1), order[:, 8]])
    angle = angle[:, order].astype(np.float64)
    cosine, sine = np.cos(angle).astype(one), np.sin(angle).astype(one)

    def parts(value):
        high = value.astype(ml_dtypes.bfloat16)
        return high, (value - high.astype(one)).astype(ml_dtypes.bfloat16)

    extra = np.zeros((8, C), one)
    extra[0] = 1.0
    synth = np.concatenate([cosine, sine, extra], 0) / one(C)
    high, low = parts(synth)
    synth = np.concatenate([high[:, :MAIN], high[:, :MAIN], low[:, :MAIN], high[:, MAIN:], high[:, MAIN:], low[:, MAIN:]], 1)
    high, low = parts(np.concatenate([cosine.T, sine.T], 1))
    forward = np.concatenate([high, high, low], 1)
    turn = np.zeros((H, H), one)
    turn[np.arange(H), (-np.arange(H)) % H] = 1.0
    turn = np.concatenate([turn] * 3, 1).astype(ml_dtypes.bfloat16)
    return synth, forward, turn


def split(value):
    high = value.astype(BF16)
    return high, (value - high.astype(F32)).astype(BF16)


def dot(left, right):
    return jnp.dot(left, right, preferred_element_type=F32)


def sub_iota():
    return lax.broadcasted_iota(jnp.int32, (8, 128), 0)


def lane_iota():
    return lax.broadcasted_iota(jnp.int32, (8, 128), 1)


def swap_pairs(tiles):
    rows = sub_iota()
    low, even = rows < 4, (rows & 2) == 0
    a0, a1, a2, a3 = tiles
    b0 = jnp.where(low, a0, pltpu.roll(a2, 4, 0))
    b1 = jnp.where(low, a1, pltpu.roll(a3, 4, 0))
    b2 = jnp.where(low, pltpu.roll(a0, 4, 0), a2)
    b3 = jnp.where(low, pltpu.roll(a1, 4, 0), a3)
    return (
        jnp.where(even, b0, pltpu.roll(b1, 2, 0)),
        jnp.where(even, pltpu.roll(b0, 6, 0), b1),
        jnp.where(even, b2, pltpu.roll(b3, 2, 0)),
        jnp.where(even, pltpu.roll(b2, 6, 0), b3),
    )


def beam_start(offsets_ref, beam):
    return offsets_ref[beam] - lax.axis_index("sky") * (CHAN * F)


def weight_rows(w_ref, i, beam):
    back = lax.rem(8 - beam, 8)
    rows = []
    for k in range(4):
        two = pltpu.roll(w_ref[pl.ds(pl.multiple_of(i * 32 + k * 8, 8), 8), :], back, 0)
        rows += [jnp.broadcast_to(two[r : r + 1], (8, 128)) for r in (0, 4)]
    return rows


def pair_rows(rows):
    at = sub_iota()
    return jnp.where(at < 4, jnp.where(at < 2, rows[0], rows[1]), jnp.where(at < 6, rows[2], rows[3]))


def combine_kernel(offsets_ref, x_ref, x9_ref, w_ref, o_ref, o9_ref, ow_ref):
    beam = pl.program_id(0)

    @pl.when(beam == 0)
    def _():
        o_ref[...] = jnp.zeros_like(o_ref)
        o9_ref[...] = jnp.zeros_like(o9_ref)
        ow_ref[...] = jnp.zeros_like(ow_ref)

    start = beam_start(offsets_ref, beam)
    whole, shift = start // 128, start % 128
    tile, part = whole // 4, (whole % 4) * 2
    lanes, rows = lane_iota(), sub_iota()
    stays = lanes >= shift
    below = rows >= part
    zero = jnp.zeros((8, 128), F32)

    def narrow(value, last_shift, last_turn):
        rolled = pltpu.roll(value, shift, 1)
        moved = pltpu.roll(rolled, 2, 0)
        joined = jnp.where(stays, rolled, jnp.where(rows >= 2, moved, last_shift))
        turned = pltpu.roll(joined, part, 0)
        return jnp.where(below, turned, last_turn), (moved, turned)

    def step(i, carry):
        last, carry9, carry_w = carry
        blocks_at, tiles_at = pl.ds(whole + i * 8, 8), pl.ds(tile + i * 2, 2)
        weights = weight_rows(w_ref, i, beam)
        wide, thin, thin_w = [], [], []
        for half in range(2):
            row = pl.ds(pl.multiple_of((i * 2 + half) * 8, 8), 8)
            pair = pair_rows(weights[half * 4 : half * 4 + 4])
            added, carry9 = narrow(x9_ref[0, 0, row, :] * pair, *carry9)
            thin.append(added)
            added, carry_w = narrow(pair, *carry_w)
            thin_w.append(added)
            blocks = [swap_pairs([x_ref[0, 4 * g + k, row, :] for k in range(4)]) for g in range(2)]
            for k in range(4):
                rolled = [pltpu.roll(blocks[g][k] * weights[half * 4 + k], shift, 1) for g in range(2)]
                wide.append(jnp.concatenate([jnp.where(stays, rolled[g], last[g]) for g in range(2)], 0))
                last = rolled
        o_ref[blocks_at] += jnp.stack(wide)
        o9_ref[tiles_at] += jnp.stack(thin)
        ow_ref[tiles_at] += jnp.stack(thin_w)
        return last, carry9, carry_w

    last, carry9, carry_w = lax.fori_loop(
        0, 16, step, ([zero, zero], (zero, zero), (zero, zero)), unroll=UNROLL
    )
    for g in range(2):
        o_ref[whole + 128, 8 * g : 8 * g + 8] += jnp.where(stays, 0.0, last[g])
    o9_ref[tile + 32] += narrow(zero, *carry9)[0]
    ow_ref[tile + 32] += narrow(zero, *carry_w)[0]


def gather_kernel(offsets_ref, r_ref, r9_ref, w_ref, d_ref, o_ref, od_ref):
    beam = pl.program_id(0)
    start = beam_start(offsets_ref, beam)
    tail = lax.axis_index("sky") == SKY - 1
    end = jnp.where(tail, CHAN * CHUNKS, 2 * CHAN * CHUNKS)
    whole, shift = start // 128, start % 128
    tile, part = whole // 4, (whole % 4) * 2
    lanes, rows = lane_iota(), sub_iota()
    stays = lanes < 128 - shift
    above = rows < 8 - part
    back = (128 - shift) % 128
    turn = (8 - part) % 8

    def block(at, g):
        value = r_ref[at, 8 * g : 8 * g + 8]
        return pltpu.roll(jnp.where(at < end, value, 0.0), back, 1)

    def turned9(at):
        return pltpu.roll(jnp.where(at * 4 < end, r9_ref[at], 0.0), turn, 0)

    def rolled9(first, second):
        return pltpu.roll(jnp.where(above, first, second), back, 1)

    first = turned9(tile)
    second = turned9(tile + 1)

    def step(i, carry):
        now, rolled, turned = carry
        weights = weight_rows(w_ref, i, beam)
        for half in range(2):
            at = i * 2 + half
            row = pl.ds(pl.multiple_of(at * 8, 8), 8)
            beyond = turned9(jnp.minimum(tile + at + 2, 63))
            after = rolled9(turned, beyond)
            moved = jnp.where(rows < 6, pltpu.roll(rolled, 6, 0), pltpu.roll(after, 6, 0))
            o_ref[0, 8, row, :] = jnp.where(stays, rolled, moved) * pair_rows(weights[half * 4 : half * 4 + 4])
            rolled, turned = after, beyond
            results = [[], []]
            for k in range(4):
                later = [block(whole + at * 4 + k + 1, g) for g in range(2)]
                for g in range(2):
                    results[g].append(jnp.where(stays, now[g], later[g]) * weights[half * 4 + k])
                now = later
            for g in range(2):
                for k, value in enumerate(swap_pairs(results[g])):
                    o_ref[0, 4 * g + k, row, :] = value
        return now, rolled, turned

    init = ([block(whole, g) for g in range(2)], rolled9(first, second), second)
    lax.fori_loop(0, 16, step, init, unroll=UNROLL)
    od_ref[...] = d_ref[...]


def exchange_kernel(
    num, num9, wsum, synth, forward, turn, res, res9, depth,
    hx, hx9, hw, sb, sb9, rx, rx_up, rx9, bk, bk9, flat, rhs_c, rhs_f, model_re, model_im,
    up_send, up_recv, up9_send, up9_recv, upw_send, upw_recv,
    to_send, to_recv, to9_send, to9_recv,
    back_send, back_recv, back9_send, back9_recv,
    down_send, down_recv, down9_send, down9_recv, ready,
):
    sky, me = lax.axis_index("sky"), lax.axis_index("chan")
    up, down = lax.rem(sky + 1, SKY), lax.rem(sky + SKY - 1, SKY)
    mine = pl.ds(pl.multiple_of(me * 8, 8), 8)

    barrier = pltpu.get_barrier_semaphore()

    def greet(d, carry):
        pl.semaphore_signal(barrier, inc=1, device_id=(sky, lax.rem(me + d, CHAN)), device_id_type=MESH)
        return carry

    lax.fori_loop(1, CHAN, greet, 0)
    for other in (up, down):
        pl.semaphore_signal(barrier, inc=1, device_id=(other, me), device_id_type=MESH)
    pl.semaphore_wait(barrier, CHAN + 1)
    pl.semaphore_signal(ready, inc=1, device_id=(down, me), device_id_type=MESH)

    def remote(src, dst, send, recv, device):
        return pltpu.make_async_remote_copy(
            src_ref=src, dst_ref=dst, send_sem=send, recv_sem=recv, device_id=device, device_id_type=MESH
        )

    second = pl.ds(CHAN, CHAN)
    up_w = remote(wsum.at[CHAN + me], hw, upw_send, upw_recv, (up, me))
    up_9 = remote(num9.at[second], hx9, up9_send, up9_recv, (up, me))

    def up_copy(s):
        return remote(num.at[second, s], hx.at[:, s], up_send.at[s], up_recv.at[s], (up, me))

    first = pl.ds(0, CHAN)
    all_sent = pl.ds(0, CHAN - 1)

    def down_copy(s):
        return remote(res.at[first, s], res.at[second, s], down_send.at[s], down_recv.at[s], (down, me))

    def among(s, chunks):
        return functools.reduce(jnp.logical_or, [s == k for k in chunks], s < 0)

    def to_all(copies):
        def send(d, carry):
            to = lax.rem(me + d, CHAN)
            for src, dst, send_sem, recv_sem, row in copies:
                remote(src(to), dst, send_sem, recv_sem, (row, to)).start()
            return carry

        lax.fori_loop(1, CHAN, send, 0)

    relayed = [s for s in range(CHUNKS) if s not in STRAIGHT_UP]
    up_copy(relayed[0]).start()
    up_9.start()
    up_w.start()
    for s in relayed[1:]:
        up_copy(s).start()

    def spread(s):
        @pl.when(jnp.logical_not(among(s, STRAIGHT_UP)))
        def _():
            up_copy(s).wait_recv()
            sb[s] = num[:CHAN, s] + jnp.where(sky > 0, hx[:, s], 0.0)
            pltpu.make_async_copy(sb.at[s, me], rx.at[s, me], to_recv.at[s]).start()
            to_all([(lambda to: sb.at[s, to], rx.at[s, me], to_send.at[s], to_recv.at[s], sky)])

    def straight_own(s):
        pltpu.make_async_copy(num.at[me, s], rx.at[s, me], to_recv.at[s]).start()
        to_all([(lambda to: num.at[to, s], rx.at[s, me], to_send.at[s], to_recv.at[s], sky)])

    def straight_up(s):
        remote(num.at[CHAN + me, s], rx_up.at[s, me], up_send.at[s], up_recv.at[s], (up, me)).start()
        to_all([(lambda to: num.at[CHAN + to, s], rx_up.at[s, me], up_send.at[s], up_recv.at[s], up)])

    def spread9():
        up_9.wait_recv()
        up_w.wait_recv()
        sb9[...] = num9[:CHAN] + jnp.where(sky > 0, hx9[...], 0.0)
        pltpu.make_async_copy(sb9.at[me], rx9.at[mine], to9_recv).start()

        to_all([(lambda to: sb9.at[to], rx9.at[mine], to9_send, to9_recv, sky)])

    is_zero = lax.broadcasted_iota(jnp.int32, (H, 128), 0) == 0

    def synthesis(field):
        high, low = split(field)
        rhs_c[0:MAIN] = high[:MAIN]
        rhs_c[MAIN : 2 * MAIN] = low[:MAIN]
        rhs_c[2 * MAIN : 3 * MAIN] = high[:MAIN]
        rhs_c[3 * MAIN : 3 * MAIN + 32] = high[MAIN:]
        rhs_c[3 * MAIN + 32 : 3 * MAIN + 64] = low[MAIN:]
        rhs_c[3 * MAIN + 64 : 3 * MAIN + 96] = high[MAIN:]
        out = dot(synth[...], rhs_c[...])
        cos_q, cos_u = out[:H, :128], out[:H, 128:]
        sin_q, sin_u = out[H:F, :128], out[H:F, 128:]
        plus_re = jnp.where(is_zero, out[F : F + 1, :128], cos_q + sin_u)
        plus_im = jnp.where(is_zero, out[F : F + 1, 128:], cos_u - sin_q)
        return plus_re, plus_im, cos_q - sin_u, cos_u + sin_q

    def residual():
        plus_re, plus_im = model_re[:H], model_im[:H]
        minus_re, minus_im = model_re[H:], model_im[H:]
        zero_re, zero_im = plus_re[0:1], plus_im[0:1]
        plus_re = jnp.where(is_zero, 0.0, plus_re)
        plus_im = jnp.where(is_zero, 0.0, plus_im)

        def put(value, row, column):
            high, low = split(value)
            columns = slice(column, column + 128)
            rhs_f[row : row + H, columns] = high
            rhs_f[F + row : F + row + H, columns] = low
            rhs_f[2 * F + row : 2 * F + row + H, columns] = high

        put(plus_re + minus_re, 0, 0)
        put(plus_im + minus_im, 0, 128)
        put(minus_im - plus_im, H, 0)
        put(plus_re - minus_re, H, 128)
        seen = dot(forward[...], rhs_f[...])
        return flat[...] - (seen + jnp.concatenate([zero_re, zero_im], 1))

    def deconvolve(s):
        pltpu.make_async_copy(rx.at[s], rx.at[s], to_recv.at[s]).wait()
        scale = wsum[me] + jnp.where(sky > 0, hw[...], 0.0) + COMBINE_FLOOR
        rows = lax.broadcasted_iota(jnp.int32, (8, 128), 0)
        scale = 1.0 / jnp.sum(jnp.where(rows == 2 * s, scale, 0.0), axis=0, keepdims=True)

        @pl.when(among(s, STRAIGHT_UP))
        def _():
            pltpu.make_async_copy(rx_up.at[s], rx_up.at[s], up_recv.at[s]).wait()
            rx[s] += jnp.where(sky > 0, rx_up[s], 0.0)

        for q in range(2):
            columns = slice(128 * q, 128 * q + 128)
            flat[:MAIN, columns] = rx[s, :, pl.ds(q, 8, stride=2), :].reshape(MAIN, 128) * scale
            flat[MAIN:, columns] = rx9[pl.ds(2 * s + q, CHAN, stride=8), :] * scale
        dirty = synthesis(flat[...])
        re = jnp.concatenate([dirty[0], dirty[2]], 0)
        im = jnp.concatenate([dirty[1], dirty[3]], 0)
        mag = jnp.sqrt(re * re + im * im)
        thresh = THRESH_FRAC * jnp.max(mag, axis=0, keepdims=True) + THRESH_BASE
        mag = STEP_GAIN * mag
        factor = STEP_GAIN * (jnp.maximum(mag - thresh, 0.0) / jnp.maximum(mag, thresh))
        model_re[...] = re * factor
        model_im[...] = im * factor

        def iteration(_, carry):
            grown = synthesis(residual())
            for plus in range(2):
                part = slice(H * plus, H * plus + H)
                re = model_re[part] + STEP_GAIN * grown[2 * plus]
                im = model_im[part] + STEP_GAIN * grown[2 * plus + 1]
                mag = jnp.sqrt(re * re + im * im)
                factor = jnp.maximum(mag - thresh, 0.0) / jnp.maximum(mag, thresh)
                model_re[part] = re * factor
                model_im[part] = im * factor
            return carry

        lax.fori_loop(0, ITERS - 1, iteration, 0)
        rest = residual()
        for q in range(2):
            columns = slice(128 * q, 128 * q + 128)
            bk[s, :, pl.ds(q, 8, stride=2), :] = rest[:MAIN, columns].reshape(CHAN, 8, 128)
            bk9[pl.ds(2 * s + q, CHAN, stride=8), :] = rest[MAIN:, columns]
        pltpu.make_async_copy(bk.at[s, me], res.at[me, s], back_recv.at[s]).start()
        straight = among(s, STRAIGHT_DOWN)
        own = (lambda to: bk.at[s, to], res.at[me, s], back_send.at[s], back_recv.at[s], sky)

        @pl.when(straight)
        def _():
            remote(bk.at[s, me], res.at[CHAN + me, s], down_send.at[s], down_recv.at[s], (down, me)).start()
            to_all([(lambda to: bk.at[s, to], res.at[CHAN + me, s], down_send.at[s], down_recv.at[s], down), own])

        @pl.when(jnp.logical_not(straight))
        def _():
            to_all([own])

        lanes = pl.ds(pl.multiple_of(s * 128, 128), 128)
        depth[0, 0:H, lanes] = model_re[H:]
        depth[1, 0:H, lanes] = model_im[H:]
        plus = jnp.concatenate([model_re[:H], model_im[:H]], 1)
        high = plus.astype(BF16)
        plus = plus - high.astype(F32)
        middle = plus.astype(BF16)
        low = (plus - middle.astype(F32)).astype(BF16)
        rhs_f[0:H] = high
        rhs_f[H : 2 * H] = middle
        rhs_f[2 * H : 3 * H] = low
        turned = dot(turn[...], rhs_f[0 : 3 * H])
        depth[0, H:, lanes] = turned[:, :128]
        depth[1, H:, lanes] = turned[:, 128:]

    def send_back9():
        pltpu.make_async_copy(bk9.at[mine], res9.at[me], back9_recv).start()
        remote(bk9.at[mine], res9.at[CHAN + me], down9_send, down9_recv, (down, me)).start()

        def row(to):
            return bk9.at[pl.ds(pl.multiple_of(to * 8, 8), 8)]

        to_all([
            (row, res9.at[CHAN + me], down9_send, down9_recv, down),
            (row, res9.at[me], back9_send, back9_recv, sky),
        ])

    for s in STRAIGHT_UP:
        straight_own(s)
    pl.semaphore_wait(ready, 1)

    def step(i, carry):
        @pl.when(i < CHUNKS)
        def _():
            spread(i)

        @pl.when(i == 0)
        def _():
            spread9()

        @pl.when(i == 1)
        def _():
            for s in STRAIGHT_UP:
                straight_up(s)

        @pl.when(i == 1)
        def _():
            pltpu.make_async_copy(rx9, rx9, to9_recv).wait()

        @pl.when((i >= 1) & (i <= CHUNKS))
        def _():
            deconvolve(i - 1)

        @pl.when(i == CHUNKS)
        def _():
            send_back9()

        @pl.when((i >= 2) & jnp.logical_not(among(i - 2, STRAIGHT_DOWN)))
        def _():
            s = i - 2
            pltpu.make_async_copy(bk.at[s], bk.at[s], back_recv.at[s]).wait()
            down_copy(s).start()

        return carry

    lax.fori_loop(0, CHUNKS + 2, step, 0)

    for s in range(CHUNKS):
        for buffer, sem in ((num, up_send), (res, down_send)):
            pltpu.make_async_copy(buffer.at[second, s], buffer.at[second, s], sem.at[s]).wait()
        for sem in (to_send, back_send):
            pltpu.make_async_copy(sb.at[s, all_sent], sb.at[s, all_sent], sem.at[s]).wait()
        if s in STRAIGHT_DOWN:
            pltpu.make_async_copy(bk.at[s], bk.at[s], back_recv.at[s]).wait()
        pltpu.make_async_copy(res.at[second, s], res.at[second, s], down_recv.at[s]).wait()
    up_w.wait_send()
    up_9.wait_send()
    for sem in (to9_send, back9_send):
        pltpu.make_async_copy(sb9.at[all_sent], sb9.at[all_sent], sem).wait()
    for sem in (back9_recv, down9_send, down9_recv):
        pltpu.make_async_copy(hx9, hx9, sem).wait()


def body(beam_images, beam_weights, offsets):
    synth, forward, turn = tables()
    images = beam_images.reshape(4, 2, PER, 128, 128).transpose(0, 2, 3, 1, 4).reshape(4, PER, 256, 128)
    weights = beam_weights.reshape(4, 128, 128).transpose(1, 0, 2).reshape(512, 128)
    shape = jax.ShapeDtypeStruct

    num, num9, wsum = pl.pallas_call(
        combine_kernel,
        grid_spec=pltpu.PrefetchScalarGridSpec(
            num_scalar_prefetch=1,
            grid=(BEAMS_DEV,),
            in_specs=[
                pl.BlockSpec((1, 8, 256, 128), lambda b, _: (b, 0, 0, 0)),
                pl.BlockSpec((1, 1, 256, 128), lambda b, _: (b, 8, 0, 0)),
                pl.BlockSpec((512, 128), lambda b, _: (0, 0)),
            ],
            out_specs=[
                pl.BlockSpec((256, 16, 128), lambda b, _: (0, 0, 0)),
                pl.BlockSpec((64, 8, 128), lambda b, _: (0, 0, 0)),
                pl.BlockSpec((64, 8, 128), lambda b, _: (0, 0, 0)),
            ],
        ),
        out_shape=[shape((256, 16, 128), F32), shape((64, 8, 128), F32), shape((64, 8, 128), F32)],
        compiler_params=pltpu.CompilerParams(vmem_limit_bytes=VMEM_LIMIT),
    )(offsets, images, images, weights)

    dma = pltpu.SemaphoreType.DMA
    vmem = pltpu.VMEM
    whole = pl.BlockSpec(memory_space=vmem)
    res, res9, depth = pl.pallas_call(
        exchange_kernel,
        in_specs=[whole] * 6,
        out_specs=[whole] * 3,
        out_shape=[
            shape((2 * CHAN, CHUNKS, 16, 128), F32),
            shape((2 * CHAN, 8, 128), F32),
            shape((2, F, F), F32),
        ],
        scratch_shapes=[
            vmem((CHAN, CHUNKS, 16, 128), F32),
            vmem((CHAN, 8, 128), F32),
            vmem((8, 128), F32),
            vmem((CHUNKS, CHAN, 16, 128), F32),
            vmem((CHAN, 8, 128), F32),
            vmem((CHUNKS, CHAN, 16, 128), F32),
            vmem((CHUNKS, CHAN, 16, 128), F32),
            vmem((CHAN * 8, 128), F32),
            vmem((CHUNKS, CHAN, 16, 128), F32),
            vmem((CHAN * 8, 128), F32),
            vmem((C, 256), F32),
            vmem((3 * C, 256), BF16),
            vmem((3 * F, 256), BF16),
            vmem((F, 128), F32),
            vmem((F, 128), F32),
            dma((CHUNKS,)), dma((CHUNKS,)), dma, dma, dma, dma,
            dma((CHUNKS,)), dma((CHUNKS,)), dma, dma,
            dma((CHUNKS,)), dma((CHUNKS,)), dma, dma,
            dma((CHUNKS,)), dma((CHUNKS,)), dma, dma,
            pltpu.SemaphoreType.REGULAR,
        ],
        compiler_params=pltpu.CompilerParams(collective_id=0, has_side_effects=True, vmem_limit_bytes=VMEM_LIMIT),
    )(num.reshape(2 * CHAN, CHUNKS, 16, 128), num9, wsum, jnp.asarray(synth), jnp.asarray(forward), jnp.asarray(turn))

    out, depth = pl.pallas_call(
        gather_kernel,
        grid_spec=pltpu.PrefetchScalarGridSpec(
            num_scalar_prefetch=1,
            grid=(BEAMS_DEV,),
            in_specs=[
                pl.BlockSpec((256, 16, 128), lambda b, _: (0, 0, 0)),
                pl.BlockSpec((64, 8, 128), lambda b, _: (0, 0, 0)),
                pl.BlockSpec((512, 128), lambda b, _: (0, 0)),
                pl.BlockSpec((2, F // 4, F), lambda b, _: (0, b, 0)),
            ],
            out_specs=[
                pl.BlockSpec((1, PER, 256, 128), lambda b, _: (b, 0, 0, 0)),
                pl.BlockSpec((2, F // 4, F), lambda b, _: (0, b, 0)),
            ],
        ),
        out_shape=[shape((BEAMS_DEV, PER, 256, 128), F32), shape((2, F, F), F32)],
        compiler_params=pltpu.CompilerParams(vmem_limit_bytes=VMEM_LIMIT),
    )(offsets, res.reshape(256, 16, 128), res9, weights, depth)
    out = out.reshape(4, PER, 128, 2, 128).transpose(0, 3, 1, 2, 4).reshape(4, 2, PER, 128 * 128)
    return out, depth


def solution(mesh):
    return jax.shard_map(
        body,
        mesh=mesh,
        in_specs=(P("sky", None, "chan", None), P("sky", None), P("sky")),
        out_specs=(P("sky", None, "chan", None), P(None, None, ("sky", "chan"))),
        check_vma=False,
    )
```

```python
import functools

import jax
import jax.numpy as jnp
import ml_dtypes
import numpy as np
from jax import lax
from jax.experimental import pallas as pl
from jax.experimental.pallas import tpu as pltpu
from jax.sharding import PartitionSpec as P

C = 288
F = 512
H = F // 2
BEAMS_DEV = 4
ITERS = 3
SKY = 8
CHAN = 32
PER = C // CHAN
MAIN = CHAN * 8
CHUNKS = 4

BAND_LOW = 800000000.0
BAND_WIDTH = 288000000.0
LIGHT = 299792458.0
DEPTH_STEP = 20.0
COMBINE_FLOOR = 0.5
THRESH_FRAC = 0.25
THRESH_BASE = 0.005
STEP_GAIN = 0.5
MESH = pl.DeviceIdType.MESH
F32 = jnp.float32
BF16 = jnp.bfloat16
VMEM_LIMIT = 56 << 20
UNROLL = 8
STRAIGHT_UP = ()
STRAIGHT_DOWN = (3,)


def tables():
    one = np.float32
    channel = np.arange(C, dtype=one)
    freq = one(BAND_LOW) + (channel + one(0.5)) * one(BAND_WIDTH / C)
    lam = one(LIGHT) / freq
    lam_sq = lam * lam
    lam_sq = lam_sq - np.mean(lam_sq, dtype=one)
    depth = (H - np.arange(H, dtype=one)) * one(DEPTH_STEP)
    angle = (one(2.0) * depth)[:, None] * lam_sq[None, :]
    order = np.arange(C).reshape(CHAN, PER)
    order = np.concatenate([order[:, :8].reshape(-1), order[:, 8]])
    angle = angle[:, order].astype(np.float64)
    cosine, sine = np.cos(angle).astype(one), np.sin(angle).astype(one)

    def parts(value):
        high = value.astype(ml_dtypes.bfloat16)
        return high, (value - high.astype(one)).astype(ml_dtypes.bfloat16)

    extra = np.zeros((8, C), one)
    extra[0] = 1.0
    synth = np.concatenate([cosine, sine, extra], 0) / one(C)
    high, low = parts(synth)
    synth = np.concatenate([high[:, :MAIN], high[:, :MAIN], low[:, :MAIN], high[:, MAIN:], high[:, MAIN:], low[:, MAIN:]], 1)
    high, low = parts(np.concatenate([cosine.T, sine.T], 1))
    forward = np.concatenate([high, high, low], 1)
    turn = np.zeros((H, H), one)
    turn[np.arange(H), (-np.arange(H)) % H] = 1.0
    turn = np.concatenate([turn] * 3, 1).astype(ml_dtypes.bfloat16)
    return synth, forward, turn


def pin(value):
    return pltpu.with_memory_space_constraint(value, pltpu.HBM)


def split(value):
    high = value.astype(BF16)
    return high, (value - high.astype(F32)).astype(BF16)


def dot(left, right):
    return jnp.dot(left, right, preferred_element_type=F32)


def sub_iota():
    return lax.broadcasted_iota(jnp.int32, (8, 128), 0)


def lane_iota():
    return lax.broadcasted_iota(jnp.int32, (8, 128), 1)


def swap_pairs(tiles):
    rows = sub_iota()
    low, even = rows < 4, (rows & 2) == 0
    a0, a1, a2, a3 = tiles
    b0 = jnp.where(low, a0, pltpu.roll(a2, 4, 0))
    b1 = jnp.where(low, a1, pltpu.roll(a3, 4, 0))
    b2 = jnp.where(low, pltpu.roll(a0, 4, 0), a2)
    b3 = jnp.where(low, pltpu.roll(a1, 4, 0), a3)
    return (
        jnp.where(even, b0, pltpu.roll(b1, 2, 0)),
        jnp.where(even, pltpu.roll(b0, 6, 0), b1),
        jnp.where(even, b2, pltpu.roll(b3, 2, 0)),
        jnp.where(even, pltpu.roll(b2, 6, 0), b3),
    )


def beam_start(offsets_ref, beam):
    return offsets_ref[beam] - lax.axis_index("sky") * (CHAN * F)


def weight_rows(w_ref, i, beam):
    back = lax.rem(8 - beam, 8)
    rows = []
    for k in range(4):
        two = pltpu.roll(w_ref[pl.ds(pl.multiple_of(i * 32 + k * 8, 8), 8), :], back, 0)
        rows += [jnp.broadcast_to(two[r : r + 1], (8, 128)) for r in (0, 4)]
    return rows


def pair_rows(rows):
    at = sub_iota()
    return jnp.where(at < 4, jnp.where(at < 2, rows[0], rows[1]), jnp.where(at < 6, rows[2], rows[3]))


def combine_kernel(offsets_ref, x_ref, x9_ref, w_ref, o_ref, o9_ref, ow_ref):
    beam = pl.program_id(0)

    @pl.when(beam == 0)
    def _():
        o_ref[...] = jnp.zeros_like(o_ref)
        o9_ref[...] = jnp.zeros_like(o9_ref)
        ow_ref[...] = jnp.zeros_like(ow_ref)

    start = beam_start(offsets_ref, beam)
    whole, shift = start // 128, start % 128
    tile, part = whole // 4, (whole % 4) * 2
    lanes, rows = lane_iota(), sub_iota()
    stays = lanes >= shift
    below = rows >= part
    zero = jnp.zeros((8, 128), F32)

    def narrow(value, last_shift, last_turn):
        rolled = pltpu.roll(value, shift, 1)
        moved = pltpu.roll(rolled, 2, 0)
        joined = jnp.where(stays, rolled, jnp.where(rows >= 2, moved, last_shift))
        turned = pltpu.roll(joined, part, 0)
        return jnp.where(below, turned, last_turn), (moved, turned)

    def step(i, carry):
        last, carry9, carry_w = carry
        blocks_at, tiles_at = pl.ds(whole + i * 8, 8), pl.ds(tile + i * 2, 2)
        weights = weight_rows(w_ref, i, beam)
        wide, thin, thin_w = [], [], []
        for half in range(2):
            row = pl.ds(pl.multiple_of((i * 2 + half) * 8, 8), 8)
            pair = pair_rows(weights[half * 4 : half * 4 + 4])
            added, carry9 = narrow(x9_ref[0, 0, row, :] * pair, *carry9)
            thin.append(added)
            added, carry_w = narrow(pair, *carry_w)
            thin_w.append(added)
            blocks = [swap_pairs([x_ref[0, 4 * g + k, row, :] for k in range(4)]) for g in range(2)]
            for k in range(4):
                rolled = [pltpu.roll(blocks[g][k] * weights[half * 4 + k], shift, 1) for g in range(2)]
                wide.append(jnp.concatenate([jnp.where(stays, rolled[g], last[g]) for g in range(2)], 0))
                last = rolled
        o_ref[blocks_at] += jnp.stack(wide)
        o9_ref[tiles_at] += jnp.stack(thin)
        ow_ref[tiles_at] += jnp.stack(thin_w)
        return last, carry9, carry_w

    last, carry9, carry_w = lax.fori_loop(
        0, 16, step, ([zero, zero], (zero, zero), (zero, zero)), unroll=UNROLL
    )
    for g in range(2):
        o_ref[whole + 128, 8 * g : 8 * g + 8] += jnp.where(stays, 0.0, last[g])
    o9_ref[tile + 32] += narrow(zero, *carry9)[0]
    ow_ref[tile + 32] += narrow(zero, *carry_w)[0]


def gather_kernel(offsets_ref, r_ref, r9_ref, w_ref, d_ref, o_ref, od_ref):
    beam = pl.program_id(0)
    start = beam_start(offsets_ref, beam)
    tail = lax.axis_index("sky") == SKY - 1
    end = jnp.where(tail, CHAN * CHUNKS, 2 * CHAN * CHUNKS)
    whole, shift = start // 128, start % 128
    tile, part = whole // 4, (whole % 4) * 2
    lanes, rows = lane_iota(), sub_iota()
    stays = lanes < 128 - shift
    above = rows < 8 - part
    back = (128 - shift) % 128
    turn = (8 - part) % 8

    def block(at, g):
        value = r_ref[at, 8 * g : 8 * g + 8]
        return pltpu.roll(jnp.where(at < end, value, 0.0), back, 1)

    def turned9(at):
        return pltpu.roll(jnp.where(at * 4 < end, r9_ref[at], 0.0), turn, 0)

    def rolled9(first, second):
        return pltpu.roll(jnp.where(above, first, second), back, 1)

    first = turned9(tile)
    second = turned9(tile + 1)

    def step(i, carry):
        now, rolled, turned = carry
        weights = weight_rows(w_ref, i, beam)
        for half in range(2):
            at = i * 2 + half
            row = pl.ds(pl.multiple_of(at * 8, 8), 8)
            beyond = turned9(jnp.minimum(tile + at + 2, 63))
            after = rolled9(turned, beyond)
            moved = jnp.where(rows < 6, pltpu.roll(rolled, 6, 0), pltpu.roll(after, 6, 0))
            o_ref[0, 8, row, :] = jnp.where(stays, rolled, moved) * pair_rows(weights[half * 4 : half * 4 + 4])
            rolled, turned = after, beyond
            results = [[], []]
            for k in range(4):
                later = [block(whole + at * 4 + k + 1, g) for g in range(2)]
                for g in range(2):
                    results[g].append(jnp.where(stays, now[g], later[g]) * weights[half * 4 + k])
                now = later
            for g in range(2):
                for k, value in enumerate(swap_pairs(results[g])):
                    o_ref[0, 4 * g + k, row, :] = value
        return now, rolled, turned

    init = ([block(whole, g) for g in range(2)], rolled9(first, second), second)
    lax.fori_loop(0, 16, step, init, unroll=UNROLL)
    od_ref[...] = d_ref[...]


def exchange_kernel(
    num, num9, wsum, synth, forward, turn, res, res9, depth,
    hx, hx9, hw, sb, sb9, rx, rx_up, rx9, bk, bk9, flat, rhs_c, rhs_f, model_re, model_im,
    up_send, up_recv, up9_send, up9_recv, upw_send, upw_recv,
    to_send, to_recv, to9_send, to9_recv,
    back_send, back_recv, back9_send, back9_recv,
    down_send, down_recv, down9_send, down9_recv, ready,
):
    sky, me = lax.axis_index("sky"), lax.axis_index("chan")
    up, down = lax.rem(sky + 1, SKY), lax.rem(sky + SKY - 1, SKY)
    mine = pl.ds(pl.multiple_of(me * 8, 8), 8)

    barrier = pltpu.get_barrier_semaphore()

    def greet(d, carry):
        pl.semaphore_signal(barrier, inc=1, device_id=(sky, lax.rem(me + d, CHAN)), device_id_type=MESH)
        return carry

    lax.fori_loop(1, CHAN, greet, 0)
    for other in (up, down):
        pl.semaphore_signal(barrier, inc=1, device_id=(other, me), device_id_type=MESH)
    pl.semaphore_wait(barrier, CHAN + 1)
    pl.semaphore_signal(ready, inc=1, device_id=(down, me), device_id_type=MESH)

    def remote(src, dst, send, recv, device):
        return pltpu.make_async_remote_copy(
            src_ref=src, dst_ref=dst, send_sem=send, recv_sem=recv, device_id=device, device_id_type=MESH
        )

    second = pl.ds(CHAN, CHAN)
    up_w = remote(wsum.at[CHAN + me], hw, upw_send, upw_recv, (up, me))
    up_9 = remote(num9.at[second], hx9, up9_send, up9_recv, (up, me))

    def up_copy(s):
        return remote(num.at[second, s], hx.at[:, s], up_send.at[s], up_recv.at[s], (up, me))

    first = pl.ds(0, CHAN)
    all_sent = pl.ds(0, CHAN - 1)

    def down_copy(s):
        return remote(res.at[first, s], res.at[second, s], down_send.at[s], down_recv.at[s], (down, me))

    def among(s, chunks):
        return functools.reduce(jnp.logical_or, [s == k for k in chunks], s < 0)

    def to_all(copies):
        def send(d, carry):
            to = lax.rem(me + d, CHAN)
            for src, dst, send_sem, recv_sem, row in copies:
                remote(src(to), dst, send_sem, recv_sem, (row, to)).start()
            return carry

        lax.fori_loop(1, CHAN, send, 0)

    relayed = [s for s in range(CHUNKS) if s not in STRAIGHT_UP]
    up_copy(relayed[0]).start()
    up_9.start()
    up_w.start()
    for s in relayed[1:]:
        up_copy(s).start()

    def spread(s):
        @pl.when(jnp.logical_not(among(s, STRAIGHT_UP)))
        def _():
            up_copy(s).wait_recv()
            sb[s] = num[:CHAN, s] + jnp.where(sky > 0, hx[:, s], 0.0)
            pltpu.make_async_copy(sb.at[s, me], rx.at[s, me], to_recv.at[s]).start()
            to_all([(lambda to: sb.at[s, to], rx.at[s, me], to_send.at[s], to_recv.at[s], sky)])

    def straight_own(s):
        pltpu.make_async_copy(num.at[me, s], rx.at[s, me], to_recv.at[s]).start()
        to_all([(lambda to: num.at[to, s], rx.at[s, me], to_send.at[s], to_recv.at[s], sky)])

    def straight_up(s):
        remote(num.at[CHAN + me, s], rx_up.at[s, me], up_send.at[s], up_recv.at[s], (up, me)).start()
        to_all([(lambda to: num.at[CHAN + to, s], rx_up.at[s, me], up_send.at[s], up_recv.at[s], up)])

    def spread9():
        up_9.wait_recv()
        up_w.wait_recv()
        sb9[...] = num9[:CHAN] + jnp.where(sky > 0, hx9[...], 0.0)
        pltpu.make_async_copy(sb9.at[me], rx9.at[mine], to9_recv).start()

        to_all([(lambda to: sb9.at[to], rx9.at[mine], to9_send, to9_recv, sky)])

    is_zero = lax.broadcasted_iota(jnp.int32, (H, 128), 0) == 0

    def synthesis(field):
        high, low = split(field)
        rhs_c[0:MAIN] = high[:MAIN]
        rhs_c[MAIN : 2 * MAIN] = low[:MAIN]
        rhs_c[2 * MAIN : 3 * MAIN] = high[:MAIN]
        rhs_c[3 * MAIN : 3 * MAIN + 32] = high[MAIN:]
        rhs_c[3 * MAIN + 32 : 3 * MAIN + 64] = low[MAIN:]
        rhs_c[3 * MAIN + 64 : 3 * MAIN + 96] = high[MAIN:]
        out = dot(synth[...], rhs_c[...])
        cos_q, cos_u = out[:H, :128], out[:H, 128:]
        sin_q, sin_u = out[H:F, :128], out[H:F, 128:]
        plus_re = jnp.where(is_zero, out[F : F + 1, :128], cos_q + sin_u)
        plus_im = jnp.where(is_zero, out[F : F + 1, 128:], cos_u - sin_q)
        return plus_re, plus_im, cos_q - sin_u, cos_u + sin_q

    def residual():
        plus_re, plus_im = model_re[:H], model_im[:H]
        minus_re, minus_im = model_re[H:], model_im[H:]
        zero_re, zero_im = plus_re[0:1], plus_im[0:1]
        plus_re = jnp.where(is_zero, 0.0, plus_re)
        plus_im = jnp.where(is_zero, 0.0, plus_im)

        def put(value, row, column):
            high, low = split(value)
            columns = slice(column, column + 128)
            rhs_f[row : row + H, columns] = high
            rhs_f[F + row : F + row + H, columns] = low
            rhs_f[2 * F + row : 2 * F + row + H, columns] = high

        put(plus_re + minus_re, 0, 0)
        put(plus_im + minus_im, 0, 128)
        put(minus_im - plus_im, H, 0)
        put(plus_re - minus_re, H, 128)
        seen = dot(forward[...], rhs_f[...])
        return flat[...] - (seen + jnp.concatenate([zero_re, zero_im], 1))

    def deconvolve(s):
        pltpu.make_async_copy(rx.at[s], rx.at[s], to_recv.at[s]).wait()
        scale = wsum[me] + jnp.where(sky > 0, hw[...], 0.0) + COMBINE_FLOOR
        rows = lax.broadcasted_iota(jnp.int32, (8, 128), 0)
        scale = 1.0 / jnp.sum(jnp.where(rows == 2 * s, scale, 0.0), axis=0, keepdims=True)

        @pl.when(among(s, STRAIGHT_UP))
        def _():
            pltpu.make_async_copy(rx_up.at[s], rx_up.at[s], up_recv.at[s]).wait()
            rx[s] += jnp.where(sky > 0, rx_up[s], 0.0)

        for q in range(2):
            columns = slice(128 * q, 128 * q + 128)
            flat[:MAIN, columns] = rx[s, :, pl.ds(q, 8, stride=2), :].reshape(MAIN, 128) * scale
            flat[MAIN:, columns] = rx9[pl.ds(2 * s + q, CHAN, stride=8), :] * scale
        dirty = synthesis(flat[...])
        re = jnp.concatenate([dirty[0], dirty[2]], 0)
        im = jnp.concatenate([dirty[1], dirty[3]], 0)
        mag = jnp.sqrt(re * re + im * im)
        thresh = THRESH_FRAC * jnp.max(mag, axis=0, keepdims=True) + THRESH_BASE
        mag = STEP_GAIN * mag
        factor = STEP_GAIN * (jnp.maximum(mag - thresh, 0.0) / jnp.maximum(mag, thresh))
        model_re[...] = re * factor
        model_im[...] = im * factor

        def iteration(_, carry):
            grown = synthesis(residual())
            for plus in range(2):
                part = slice(H * plus, H * plus + H)
                re = model_re[part] + STEP_GAIN * grown[2 * plus]
                im = model_im[part] + STEP_GAIN * grown[2 * plus + 1]
                mag = jnp.sqrt(re * re + im * im)
                factor = jnp.maximum(mag - thresh, 0.0) / jnp.maximum(mag, thresh)
                model_re[part] = re * factor
                model_im[part] = im * factor
            return carry

        lax.fori_loop(0, ITERS - 1, iteration, 0)
        rest = residual()
        for q in range(2):
            columns = slice(128 * q, 128 * q + 128)
            bk[s, :, pl.ds(q, 8, stride=2), :] = rest[:MAIN, columns].reshape(CHAN, 8, 128)
            bk9[pl.ds(2 * s + q, CHAN, stride=8), :] = rest[MAIN:, columns]
        pltpu.make_async_copy(bk.at[s, me], res.at[me, s], back_recv.at[s]).start()
        straight = among(s, STRAIGHT_DOWN)
        own = (lambda to: bk.at[s, to], res.at[me, s], back_send.at[s], back_recv.at[s], sky)

        @pl.when(straight)
        def _():
            remote(bk.at[s, me], res.at[CHAN + me, s], down_send.at[s], down_recv.at[s], (down, me)).start()
            to_all([(lambda to: bk.at[s, to], res.at[CHAN + me, s], down_send.at[s], down_recv.at[s], down), own])

        @pl.when(jnp.logical_not(straight))
        def _():
            to_all([own])

        lanes = pl.ds(pl.multiple_of(s * 128, 128), 128)
        depth[0, 0:H, lanes] = model_re[H:]
        depth[1, 0:H, lanes] = model_im[H:]
        plus = jnp.concatenate([model_re[:H], model_im[:H]], 1)
        high = plus.astype(BF16)
        plus = plus - high.astype(F32)
        middle = plus.astype(BF16)
        low = (plus - middle.astype(F32)).astype(BF16)
        rhs_f[0:H] = high
        rhs_f[H : 2 * H] = middle
        rhs_f[2 * H : 3 * H] = low
        turned = dot(turn[...], rhs_f[0 : 3 * H])
        depth[0, H:, lanes] = turned[:, :128]
        depth[1, H:, lanes] = turned[:, 128:]

    def send_back9():
        pltpu.make_async_copy(bk9.at[mine], res9.at[me], back9_recv).start()
        remote(bk9.at[mine], res9.at[CHAN + me], down9_send, down9_recv, (down, me)).start()

        def row(to):
            return bk9.at[pl.ds(pl.multiple_of(to * 8, 8), 8)]

        to_all([
            (row, res9.at[CHAN + me], down9_send, down9_recv, down),
            (row, res9.at[me], back9_send, back9_recv, sky),
        ])

    for s in STRAIGHT_UP:
        straight_own(s)
    pl.semaphore_wait(ready, 1)

    def step(i, carry):
        @pl.when(i < CHUNKS)
        def _():
            spread(i)

        @pl.when(i == 0)
        def _():
            spread9()

        @pl.when(i == 1)
        def _():
            for s in STRAIGHT_UP:
                straight_up(s)

        @pl.when(i == 1)
        def _():
            pltpu.make_async_copy(rx9, rx9, to9_recv).wait()

        @pl.when((i >= 1) & (i <= CHUNKS))
        def _():
            deconvolve(i - 1)

        @pl.when(i == CHUNKS)
        def _():
            send_back9()

        @pl.when((i >= 2) & jnp.logical_not(among(i - 2, STRAIGHT_DOWN)))
        def _():
            s = i - 2
            pltpu.make_async_copy(bk.at[s], bk.at[s], back_recv.at[s]).wait()
            down_copy(s).start()

        return carry

    lax.fori_loop(0, CHUNKS + 2, step, 0)

    for s in range(CHUNKS):
        for buffer, sem in ((num, up_send), (res, down_send)):
            pltpu.make_async_copy(buffer.at[second, s], buffer.at[second, s], sem.at[s]).wait()
        for sem in (to_send, back_send):
            pltpu.make_async_copy(sb.at[s, all_sent], sb.at[s, all_sent], sem.at[s]).wait()
        if s in STRAIGHT_DOWN:
            pltpu.make_async_copy(bk.at[s], bk.at[s], back_recv.at[s]).wait()
        pltpu.make_async_copy(res.at[second, s], res.at[second, s], down_recv.at[s]).wait()
    up_w.wait_send()
    up_9.wait_send()
    for sem in (to9_send, back9_send):
        pltpu.make_async_copy(sb9.at[all_sent], sb9.at[all_sent], sem).wait()
    for sem in (back9_recv, down9_send, down9_recv):
        pltpu.make_async_copy(hx9, hx9, sem).wait()


def body(beam_images, beam_weights, offsets):
    synth, forward, turn = tables()
    images = beam_images.reshape(4, 2, PER, 128, 128).transpose(0, 2, 3, 1, 4).reshape(4, PER, 256, 128)
    weights = beam_weights.reshape(4, 128, 128).transpose(1, 0, 2).reshape(512, 128)
    shape = jax.ShapeDtypeStruct

    num, num9, wsum = pl.pallas_call(
        combine_kernel,
        grid_spec=pltpu.PrefetchScalarGridSpec(
            num_scalar_prefetch=1,
            grid=(BEAMS_DEV,),
            in_specs=[
                pl.BlockSpec((1, 8, 256, 128), lambda b, _: (b, 0, 0, 0)),
                pl.BlockSpec((1, 1, 256, 128), lambda b, _: (b, 8, 0, 0)),
                pl.BlockSpec((512, 128), lambda b, _: (0, 0)),
            ],
            out_specs=[
                pl.BlockSpec((256, 16, 128), lambda b, _: (0, 0, 0)),
                pl.BlockSpec((64, 8, 128), lambda b, _: (0, 0, 0)),
                pl.BlockSpec((64, 8, 128), lambda b, _: (0, 0, 0)),
            ],
        ),
        out_shape=[shape((256, 16, 128), F32), shape((64, 8, 128), F32), shape((64, 8, 128), F32)],
        compiler_params=pltpu.CompilerParams(vmem_limit_bytes=14 << 20),
    )(pin(offsets), pin(images), pin(images), pin(weights))

    dma = pltpu.SemaphoreType.DMA
    vmem = pltpu.VMEM
    whole = pl.BlockSpec(memory_space=vmem)
    res, res9, depth = pl.pallas_call(
        exchange_kernel,
        in_specs=[whole] * 6,
        out_specs=[whole] * 3,
        out_shape=[
            shape((2 * CHAN, CHUNKS, 16, 128), F32),
            shape((2 * CHAN, 8, 128), F32),
            shape((2, F, F), F32),
        ],
        scratch_shapes=[
            vmem((CHAN, CHUNKS, 16, 128), F32),
            vmem((CHAN, 8, 128), F32),
            vmem((8, 128), F32),
            vmem((CHUNKS, CHAN, 16, 128), F32),
            vmem((CHAN, 8, 128), F32),
            vmem((CHUNKS, CHAN, 16, 128), F32),
            vmem((CHUNKS, CHAN, 16, 128), F32),
            vmem((CHAN * 8, 128), F32),
            vmem((CHUNKS, CHAN, 16, 128), F32),
            vmem((CHAN * 8, 128), F32),
            vmem((C, 256), F32),
            vmem((3 * C, 256), BF16),
            vmem((3 * F, 256), BF16),
            vmem((F, 128), F32),
            vmem((F, 128), F32),
            dma((CHUNKS,)), dma((CHUNKS,)), dma, dma, dma, dma,
            dma((CHUNKS,)), dma((CHUNKS,)), dma, dma,
            dma((CHUNKS,)), dma((CHUNKS,)), dma, dma,
            dma((CHUNKS,)), dma((CHUNKS,)), dma, dma,
            pltpu.SemaphoreType.REGULAR,
        ],
        compiler_params=pltpu.CompilerParams(collective_id=0, has_side_effects=True, vmem_limit_bytes=30 << 20),
    )(num.reshape(2 * CHAN, CHUNKS, 16, 128), num9, wsum, jnp.asarray(synth), jnp.asarray(forward), jnp.asarray(turn))

    out, depth = pl.pallas_call(
        gather_kernel,
        grid_spec=pltpu.PrefetchScalarGridSpec(
            num_scalar_prefetch=1,
            grid=(BEAMS_DEV,),
            in_specs=[
                pl.BlockSpec((256, 16, 128), lambda b, _: (0, 0, 0)),
                pl.BlockSpec((64, 8, 128), lambda b, _: (0, 0, 0)),
                pl.BlockSpec((512, 128), lambda b, _: (0, 0)),
                pl.BlockSpec((2, F // 4, F), lambda b, _: (0, b, 0)),
            ],
            out_specs=[
                pl.BlockSpec((1, PER, 256, 128), lambda b, _: (b, 0, 0, 0)),
                pl.BlockSpec((2, F // 4, F), lambda b, _: (0, b, 0)),
            ],
        ),
        out_shape=[shape((BEAMS_DEV, PER, 256, 128), F32), shape((2, F, F), F32)],
        compiler_params=pltpu.CompilerParams(vmem_limit_bytes=18 << 20),
    )(offsets, res.reshape(256, 16, 128), res9, weights, depth)
    out = out.reshape(4, PER, 128, 2, 128).transpose(0, 3, 1, 2, 4).reshape(4, 2, PER, 128 * 128)
    return out, depth


def solution(mesh):
    return jax.shard_map(
        body,
        mesh=mesh,
        in_specs=(P("sky", None, "chan", None), P("sky", None), P("sky")),
        out_specs=(P("sky", None, "chan", None), P(None, None, ("sky", "chan"))),
        check_vma=False,
    )
```

```python
import functools

import jax
import jax.numpy as jnp
import ml_dtypes
import numpy as np
from jax import lax
from jax.experimental import pallas as pl
from jax.experimental.pallas import tpu as pltpu
from jax.sharding import PartitionSpec as P

C = 288
F = 512
H = F // 2
BEAMS_DEV = 4
ITERS = 3
SKY = 8
CHAN = 32
PER = C // CHAN
MAIN = CHAN * 8
CHUNKS = 4

BAND_LOW = 800000000.0
BAND_WIDTH = 288000000.0
LIGHT = 299792458.0
DEPTH_STEP = 20.0
COMBINE_FLOOR = 0.5
THRESH_FRAC = 0.25
THRESH_BASE = 0.005
STEP_GAIN = 0.5
MESH = pl.DeviceIdType.MESH
F32 = jnp.float32
BF16 = jnp.bfloat16
VMEM_LIMIT = 56 << 20
UNROLL = 16
STRAIGHT_UP = ()
STRAIGHT_DOWN = (3,)


def tables():
    one = np.float32
    channel = np.arange(C, dtype=one)
    freq = one(BAND_LOW) + (channel + one(0.5)) * one(BAND_WIDTH / C)
    lam = one(LIGHT) / freq
    lam_sq = lam * lam
    lam_sq = lam_sq - np.mean(lam_sq, dtype=one)
    depth = (H - np.arange(H, dtype=one)) * one(DEPTH_STEP)
    angle = (one(2.0) * depth)[:, None] * lam_sq[None, :]
    order = np.arange(C).reshape(CHAN, PER)
    order = np.concatenate([order[:, :8].reshape(-1), order[:, 8]])
    angle = angle[:, order].astype(np.float64)
    cosine, sine = np.cos(angle).astype(one), np.sin(angle).astype(one)

    def parts(value):
        high = value.astype(ml_dtypes.bfloat16)
        return high, (value - high.astype(one)).astype(ml_dtypes.bfloat16)

    extra = np.zeros((8, C), one)
    extra[0] = 1.0
    synth = np.concatenate([cosine, sine, extra], 0) / one(C)
    high, low = parts(synth)
    synth = np.concatenate([high[:, :MAIN], high[:, :MAIN], low[:, :MAIN], high[:, MAIN:], high[:, MAIN:], low[:, MAIN:]], 1)
    high, low = parts(np.concatenate([cosine.T, sine.T], 1))
    forward = np.concatenate([high, high, low], 1)
    turn = np.zeros((H, H), one)
    turn[np.arange(H), (-np.arange(H)) % H] = 1.0
    turn = np.concatenate([turn] * 3, 1).astype(ml_dtypes.bfloat16)
    return synth, forward, turn


def pin(value):
    return pltpu.with_memory_space_constraint(value, pltpu.HBM)


def split(value):
    high = value.astype(BF16)
    return high, (value - high.astype(F32)).astype(BF16)


def dot(left, right):
    return jnp.dot(left, right, preferred_element_type=F32)


def sub_iota():
    return lax.broadcasted_iota(jnp.int32, (8, 128), 0)


def lane_iota():
    return lax.broadcasted_iota(jnp.int32, (8, 128), 1)


def swap_pairs(tiles):
    rows = sub_iota()
    low, even = rows < 4, (rows & 2) == 0
    a0, a1, a2, a3 = tiles
    b0 = jnp.where(low, a0, pltpu.roll(a2, 4, 0))
    b1 = jnp.where(low, a1, pltpu.roll(a3, 4, 0))
    b2 = jnp.where(low, pltpu.roll(a0, 4, 0), a2)
    b3 = jnp.where(low, pltpu.roll(a1, 4, 0), a3)
    return (
        jnp.where(even, b0, pltpu.roll(b1, 2, 0)),
        jnp.where(even, pltpu.roll(b0, 6, 0), b1),
        jnp.where(even, b2, pltpu.roll(b3, 2, 0)),
        jnp.where(even, pltpu.roll(b2, 6, 0), b3),
    )


def beam_start(offsets_ref, beam):
    return offsets_ref[beam] - lax.axis_index("sky") * (CHAN * F)


def weight_rows(w_ref, i, beam):
    back = lax.rem(8 - beam, 8)
    rows = []
    for k in range(4):
        two = pltpu.roll(w_ref[pl.ds(pl.multiple_of(i * 32 + k * 8, 8), 8), :], back, 0)
        rows += [jnp.broadcast_to(two[r : r + 1], (8, 128)) for r in (0, 4)]
    return rows


def pair_rows(rows):
    at = sub_iota()
    return jnp.where(at < 4, jnp.where(at < 2, rows[0], rows[1]), jnp.where(at < 6, rows[2], rows[3]))


def combine_kernel(offsets_ref, x_ref, x9_ref, w_ref, o_ref, o9_ref, ow_ref):
    beam = pl.program_id(0)

    @pl.when(beam == 0)
    def _():
        o_ref[...] = jnp.zeros_like(o_ref)
        o9_ref[...] = jnp.zeros_like(o9_ref)
        ow_ref[...] = jnp.zeros_like(ow_ref)

    start = beam_start(offsets_ref, beam)
    whole, shift = start // 128, start % 128
    tile, part = whole // 4, (whole % 4) * 2
    lanes, rows = lane_iota(), sub_iota()
    stays = lanes >= shift
    below = rows >= part
    zero = jnp.zeros((8, 128), F32)

    def narrow(value, last_shift, last_turn):
        rolled = pltpu.roll(value, shift, 1)
        moved = pltpu.roll(rolled, 2, 0)
        joined = jnp.where(stays, rolled, jnp.where(rows >= 2, moved, last_shift))
        turned = pltpu.roll(joined, part, 0)
        return jnp.where(below, turned, last_turn), (moved, turned)

    def step(i, carry):
        last, carry9, carry_w = carry
        blocks_at, tiles_at = pl.ds(whole + i * 8, 8), pl.ds(tile + i * 2, 2)
        weights = weight_rows(w_ref, i, beam)
        wide, thin, thin_w = [], [], []
        for half in range(2):
            row = pl.ds(pl.multiple_of((i * 2 + half) * 8, 8), 8)
            pair = pair_rows(weights[half * 4 : half * 4 + 4])
            added, carry9 = narrow(x9_ref[0, 0, row, :] * pair, *carry9)
            thin.append(added)
            added, carry_w = narrow(pair, *carry_w)
            thin_w.append(added)
            blocks = [swap_pairs([x_ref[0, 4 * g + k, row, :] for k in range(4)]) for g in range(2)]
            for k in range(4):
                rolled = [pltpu.roll(blocks[g][k] * weights[half * 4 + k], shift, 1) for g in range(2)]
                wide.append(jnp.concatenate([jnp.where(stays, rolled[g], last[g]) for g in range(2)], 0))
                last = rolled
        o_ref[blocks_at] += jnp.stack(wide)
        o9_ref[tiles_at] += jnp.stack(thin)
        ow_ref[tiles_at] += jnp.stack(thin_w)
        return last, carry9, carry_w

    last, carry9, carry_w = lax.fori_loop(
        0, 16, step, ([zero, zero], (zero, zero), (zero, zero)), unroll=UNROLL
    )
    for g in range(2):
        o_ref[whole + 128, 8 * g : 8 * g + 8] += jnp.where(stays, 0.0, last[g])
    o9_ref[tile + 32] += narrow(zero, *carry9)[0]
    ow_ref[tile + 32] += narrow(zero, *carry_w)[0]


def gather_kernel(offsets_ref, r_ref, r9_ref, w_ref, d_ref, o_ref, od_ref):
    beam = pl.program_id(0)
    start = beam_start(offsets_ref, beam)
    tail = lax.axis_index("sky") == SKY - 1
    end = jnp.where(tail, CHAN * CHUNKS, 2 * CHAN * CHUNKS)
    whole, shift = start // 128, start % 128
    tile, part = whole // 4, (whole % 4) * 2
    lanes, rows = lane_iota(), sub_iota()
    stays = lanes < 128 - shift
    above = rows < 8 - part
    back = (128 - shift) % 128
    turn = (8 - part) % 8

    def block(at, g):
        value = r_ref[at, 8 * g : 8 * g + 8]
        return pltpu.roll(jnp.where(at < end, value, 0.0), back, 1)

    def turned9(at):
        return pltpu.roll(jnp.where(at * 4 < end, r9_ref[at], 0.0), turn, 0)

    def rolled9(first, second):
        return pltpu.roll(jnp.where(above, first, second), back, 1)

    first = turned9(tile)
    second = turned9(tile + 1)

    def step(i, carry):
        now, rolled, turned = carry
        weights = weight_rows(w_ref, i, beam)
        for half in range(2):
            at = i * 2 + half
            row = pl.ds(pl.multiple_of(at * 8, 8), 8)
            beyond = turned9(jnp.minimum(tile + at + 2, 63))
            after = rolled9(turned, beyond)
            moved = jnp.where(rows < 6, pltpu.roll(rolled, 6, 0), pltpu.roll(after, 6, 0))
            o_ref[0, 8, row, :] = jnp.where(stays, rolled, moved) * pair_rows(weights[half * 4 : half * 4 + 4])
            rolled, turned = after, beyond
            results = [[], []]
            for k in range(4):
                later = [block(whole + at * 4 + k + 1, g) for g in range(2)]
                for g in range(2):
                    results[g].append(jnp.where(stays, now[g], later[g]) * weights[half * 4 + k])
                now = later
            for g in range(2):
                for k, value in enumerate(swap_pairs(results[g])):
                    o_ref[0, 4 * g + k, row, :] = value
        return now, rolled, turned

    init = ([block(whole, g) for g in range(2)], rolled9(first, second), second)
    lax.fori_loop(0, 16, step, init, unroll=UNROLL)
    od_ref[...] = d_ref[...]


def exchange_kernel(
    num, num9, wsum, synth, forward, turn, res, res9, depth,
    hx, hx9, hw, sb, sb9, rx, rx_up, rx9, bk, bk9, flat, rhs_c, rhs_f, model_re, model_im,
    up_send, up_recv, up9_send, up9_recv, upw_send, upw_recv,
    to_send, to_recv, to9_send, to9_recv,
    back_send, back_recv, back9_send, back9_recv,
    down_send, down_recv, down9_send, down9_recv, ready,
):
    sky, me = lax.axis_index("sky"), lax.axis_index("chan")
    up, down = lax.rem(sky + 1, SKY), lax.rem(sky + SKY - 1, SKY)
    mine = pl.ds(pl.multiple_of(me * 8, 8), 8)

    barrier = pltpu.get_barrier_semaphore()

    def greet(d, carry):
        pl.semaphore_signal(barrier, inc=1, device_id=(sky, lax.rem(me + d, CHAN)), device_id_type=MESH)
        return carry

    lax.fori_loop(1, CHAN, greet, 0)
    for other in (up, down):
        pl.semaphore_signal(barrier, inc=1, device_id=(other, me), device_id_type=MESH)
    pl.semaphore_wait(barrier, CHAN + 1)
    pl.semaphore_signal(ready, inc=1, device_id=(down, me), device_id_type=MESH)

    def remote(src, dst, send, recv, device):
        return pltpu.make_async_remote_copy(
            src_ref=src, dst_ref=dst, send_sem=send, recv_sem=recv, device_id=device, device_id_type=MESH
        )

    second = pl.ds(CHAN, CHAN)
    up_w = remote(wsum.at[CHAN + me], hw, upw_send, upw_recv, (up, me))
    up_9 = remote(num9.at[second], hx9, up9_send, up9_recv, (up, me))

    def up_copy(s):
        return remote(num.at[second, s], hx.at[:, s], up_send.at[s], up_recv.at[s], (up, me))

    first = pl.ds(0, CHAN)
    all_sent = pl.ds(0, CHAN - 1)

    def down_copy(s):
        return remote(res.at[first, s], res.at[second, s], down_send.at[s], down_recv.at[s], (down, me))

    def among(s, chunks):
        return functools.reduce(jnp.logical_or, [s == k for k in chunks], s < 0)

    def to_all(copies):
        def send(d, carry):
            to = lax.rem(me + d, CHAN)
            for src, dst, send_sem, recv_sem, row in copies:
                remote(src(to), dst, send_sem, recv_sem, (row, to)).start()
            return carry

        lax.fori_loop(1, CHAN, send, 0)

    relayed = [s for s in range(CHUNKS) if s not in STRAIGHT_UP]
    up_copy(relayed[0]).start()
    up_9.start()
    up_w.start()
    for s in relayed[1:]:
        up_copy(s).start()

    def spread(s):
        @pl.when(jnp.logical_not(among(s, STRAIGHT_UP)))
        def _():
            up_copy(s).wait_recv()
            sb[s] = num[:CHAN, s] + jnp.where(sky > 0, hx[:, s], 0.0)
            pltpu.make_async_copy(sb.at[s, me], rx.at[s, me], to_recv.at[s]).start()
            to_all([(lambda to: sb.at[s, to], rx.at[s, me], to_send.at[s], to_recv.at[s], sky)])

    def straight_own(s):
        pltpu.make_async_copy(num.at[me, s], rx.at[s, me], to_recv.at[s]).start()
        to_all([(lambda to: num.at[to, s], rx.at[s, me], to_send.at[s], to_recv.at[s], sky)])

    def straight_up(s):
        remote(num.at[CHAN + me, s], rx_up.at[s, me], up_send.at[s], up_recv.at[s], (up, me)).start()
        to_all([(lambda to: num.at[CHAN + to, s], rx_up.at[s, me], up_send.at[s], up_recv.at[s], up)])

    def spread9():
        up_9.wait_recv()
        up_w.wait_recv()
        sb9[...] = num9[:CHAN] + jnp.where(sky > 0, hx9[...], 0.0)
        pltpu.make_async_copy(sb9.at[me], rx9.at[mine], to9_recv).start()

        to_all([(lambda to: sb9.at[to], rx9.at[mine], to9_send, to9_recv, sky)])

    is_zero = lax.broadcasted_iota(jnp.int32, (H, 128), 0) == 0

    def synthesis(field):
        high, low = split(field)
        rhs_c[0:MAIN] = high[:MAIN]
        rhs_c[MAIN : 2 * MAIN] = low[:MAIN]
        rhs_c[2 * MAIN : 3 * MAIN] = high[:MAIN]
        rhs_c[3 * MAIN : 3 * MAIN + 32] = high[MAIN:]
        rhs_c[3 * MAIN + 32 : 3 * MAIN + 64] = low[MAIN:]
        rhs_c[3 * MAIN + 64 : 3 * MAIN + 96] = high[MAIN:]
        out = dot(synth[...], rhs_c[...])
        cos_q, cos_u = out[:H, :128], out[:H, 128:]
        sin_q, sin_u = out[H:F, :128], out[H:F, 128:]
        plus_re = jnp.where(is_zero, out[F : F + 1, :128], cos_q + sin_u)
        plus_im = jnp.where(is_zero, out[F : F + 1, 128:], cos_u - sin_q)
        return plus_re, plus_im, cos_q - sin_u, cos_u + sin_q

    def residual():
        plus_re, plus_im = model_re[:H], model_im[:H]
        minus_re, minus_im = model_re[H:], model_im[H:]
        zero_re, zero_im = plus_re[0:1], plus_im[0:1]
        plus_re = jnp.where(is_zero, 0.0, plus_re)
        plus_im = jnp.where(is_zero, 0.0, plus_im)

        def put(value, row, column):
            high, low = split(value)
            columns = slice(column, column + 128)
            rhs_f[row : row + H, columns] = high
            rhs_f[F + row : F + row + H, columns] = low
            rhs_f[2 * F + row : 2 * F + row + H, columns] = high

        put(plus_re + minus_re, 0, 0)
        put(plus_im + minus_im, 0, 128)
        put(minus_im - plus_im, H, 0)
        put(plus_re - minus_re, H, 128)
        seen = dot(forward[...], rhs_f[...])
        return flat[...] - (seen + jnp.concatenate([zero_re, zero_im], 1))

    def deconvolve(s):
        pltpu.make_async_copy(rx.at[s], rx.at[s], to_recv.at[s]).wait()
        scale = wsum[me] + jnp.where(sky > 0, hw[...], 0.0) + COMBINE_FLOOR
        rows = lax.broadcasted_iota(jnp.int32, (8, 128), 0)
        scale = 1.0 / jnp.sum(jnp.where(rows == 2 * s, scale, 0.0), axis=0, keepdims=True)

        @pl.when(among(s, STRAIGHT_UP))
        def _():
            pltpu.make_async_copy(rx_up.at[s], rx_up.at[s], up_recv.at[s]).wait()
            rx[s] += jnp.where(sky > 0, rx_up[s], 0.0)

        for q in range(2):
            columns = slice(128 * q, 128 * q + 128)
            flat[:MAIN, columns] = rx[s, :, pl.ds(q, 8, stride=2), :].reshape(MAIN, 128) * scale
            flat[MAIN:, columns] = rx9[pl.ds(2 * s + q, CHAN, stride=8), :] * scale
        dirty = synthesis(flat[...])
        re = jnp.concatenate([dirty[0], dirty[2]], 0)
        im = jnp.concatenate([dirty[1], dirty[3]], 0)
        mag = jnp.sqrt(re * re + im * im)
        thresh = THRESH_FRAC * jnp.max(mag, axis=0, keepdims=True) + THRESH_BASE
        mag = STEP_GAIN * mag
        factor = STEP_GAIN * (jnp.maximum(mag - thresh, 0.0) / jnp.maximum(mag, thresh))
        model_re[...] = re * factor
        model_im[...] = im * factor

        def iteration(_, carry):
            grown = synthesis(residual())
            for plus in range(2):
                part = slice(H * plus, H * plus + H)
                re = model_re[part] + STEP_GAIN * grown[2 * plus]
                im = model_im[part] + STEP_GAIN * grown[2 * plus + 1]
                mag = jnp.sqrt(re * re + im * im)
                factor = jnp.maximum(mag - thresh, 0.0) / jnp.maximum(mag, thresh)
                model_re[part] = re * factor
                model_im[part] = im * factor
            return carry

        lax.fori_loop(0, ITERS - 1, iteration, 0)
        rest = residual()
        for q in range(2):
            columns = slice(128 * q, 128 * q + 128)
            bk[s, :, pl.ds(q, 8, stride=2), :] = rest[:MAIN, columns].reshape(CHAN, 8, 128)
            bk9[pl.ds(2 * s + q, CHAN, stride=8), :] = rest[MAIN:, columns]
        pltpu.make_async_copy(bk.at[s, me], res.at[me, s], back_recv.at[s]).start()
        straight = among(s, STRAIGHT_DOWN)
        own = (lambda to: bk.at[s, to], res.at[me, s], back_send.at[s], back_recv.at[s], sky)

        @pl.when(straight)
        def _():
            remote(bk.at[s, me], res.at[CHAN + me, s], down_send.at[s], down_recv.at[s], (down, me)).start()
            to_all([(lambda to: bk.at[s, to], res.at[CHAN + me, s], down_send.at[s], down_recv.at[s], down), own])

        @pl.when(jnp.logical_not(straight))
        def _():
            to_all([own])

        lanes = pl.ds(pl.multiple_of(s * 128, 128), 128)
        depth[0, 0:H, lanes] = model_re[H:]
        depth[1, 0:H, lanes] = model_im[H:]
        plus = jnp.concatenate([model_re[:H], model_im[:H]], 1)
        high = plus.astype(BF16)
        plus = plus - high.astype(F32)
        middle = plus.astype(BF16)
        low = (plus - middle.astype(F32)).astype(BF16)
        rhs_f[0:H] = high
        rhs_f[H : 2 * H] = middle
        rhs_f[2 * H : 3 * H] = low
        turned = dot(turn[...], rhs_f[0 : 3 * H])
        depth[0, H:, lanes] = turned[:, :128]
        depth[1, H:, lanes] = turned[:, 128:]

    def send_back9():
        pltpu.make_async_copy(bk9.at[mine], res9.at[me], back9_recv).start()
        remote(bk9.at[mine], res9.at[CHAN + me], down9_send, down9_recv, (down, me)).start()

        def row(to):
            return bk9.at[pl.ds(pl.multiple_of(to * 8, 8), 8)]

        to_all([
            (row, res9.at[CHAN + me], down9_send, down9_recv, down),
            (row, res9.at[me], back9_send, back9_recv, sky),
        ])

    for s in STRAIGHT_UP:
        straight_own(s)
    pl.semaphore_wait(ready, 1)

    def step(i, carry):
        @pl.when(i < CHUNKS)
        def _():
            spread(i)

        @pl.when(i == 0)
        def _():
            spread9()

        @pl.when(i == 1)
        def _():
            for s in STRAIGHT_UP:
                straight_up(s)

        @pl.when(i == 1)
        def _():
            pltpu.make_async_copy(rx9, rx9, to9_recv).wait()

        @pl.when((i >= 1) & (i <= CHUNKS))
        def _():
            deconvolve(i - 1)

        @pl.when(i == CHUNKS)
        def _():
            send_back9()

        @pl.when((i >= 2) & jnp.logical_not(among(i - 2, STRAIGHT_DOWN)))
        def _():
            s = i - 2
            pltpu.make_async_copy(bk.at[s], bk.at[s], back_recv.at[s]).wait()
            down_copy(s).start()

        return carry

    lax.fori_loop(0, CHUNKS + 2, step, 0)

    for s in range(CHUNKS):
        for buffer, sem in ((num, up_send), (res, down_send)):
            pltpu.make_async_copy(buffer.at[second, s], buffer.at[second, s], sem.at[s]).wait()
        for sem in (to_send, back_send):
            pltpu.make_async_copy(sb.at[s, all_sent], sb.at[s, all_sent], sem.at[s]).wait()
        if s in STRAIGHT_DOWN:
            pltpu.make_async_copy(bk.at[s], bk.at[s], back_recv.at[s]).wait()
        pltpu.make_async_copy(res.at[second, s], res.at[second, s], down_recv.at[s]).wait()
    up_w.wait_send()
    up_9.wait_send()
    for sem in (to9_send, back9_send):
        pltpu.make_async_copy(sb9.at[all_sent], sb9.at[all_sent], sem).wait()
    for sem in (back9_recv, down9_send, down9_recv):
        pltpu.make_async_copy(hx9, hx9, sem).wait()


def body(beam_images, beam_weights, offsets):
    synth, forward, turn = tables()
    images = beam_images.reshape(4, 2, PER, 128, 128).transpose(0, 2, 3, 1, 4).reshape(4, PER, 256, 128)
    weights = beam_weights.reshape(4, 128, 128).transpose(1, 0, 2).reshape(512, 128)
    shape = jax.ShapeDtypeStruct

    num, num9, wsum = pl.pallas_call(
        combine_kernel,
        grid_spec=pltpu.PrefetchScalarGridSpec(
            num_scalar_prefetch=1,
            grid=(BEAMS_DEV,),
            in_specs=[
                pl.BlockSpec((1, 8, 256, 128), lambda b, _: (b, 0, 0, 0)),
                pl.BlockSpec((1, 1, 256, 128), lambda b, _: (b, 8, 0, 0)),
                pl.BlockSpec((512, 128), lambda b, _: (0, 0)),
            ],
            out_specs=[
                pl.BlockSpec((256, 16, 128), lambda b, _: (0, 0, 0)),
                pl.BlockSpec((64, 8, 128), lambda b, _: (0, 0, 0)),
                pl.BlockSpec((64, 8, 128), lambda b, _: (0, 0, 0)),
            ],
        ),
        out_shape=[shape((256, 16, 128), F32), shape((64, 8, 128), F32), shape((64, 8, 128), F32)],
        compiler_params=pltpu.CompilerParams(vmem_limit_bytes=14 << 20),
    )(pin(offsets), pin(images), pin(images), pin(weights))

    dma = pltpu.SemaphoreType.DMA
    vmem = pltpu.VMEM
    whole = pl.BlockSpec(memory_space=vmem)
    res, res9, depth = pl.pallas_call(
        exchange_kernel,
        in_specs=[whole] * 6,
        out_specs=[whole] * 3,
        out_shape=[
            shape((2 * CHAN, CHUNKS, 16, 128), F32),
            shape((2 * CHAN, 8, 128), F32),
            shape((2, F, F), F32),
        ],
        scratch_shapes=[
            vmem((CHAN, CHUNKS, 16, 128), F32),
            vmem((CHAN, 8, 128), F32),
            vmem((8, 128), F32),
            vmem((CHUNKS, CHAN, 16, 128), F32),
            vmem((CHAN, 8, 128), F32),
            vmem((CHUNKS, CHAN, 16, 128), F32),
            vmem((CHUNKS, CHAN, 16, 128), F32),
            vmem((CHAN * 8, 128), F32),
            vmem((CHUNKS, CHAN, 16, 128), F32),
            vmem((CHAN * 8, 128), F32),
            vmem((C, 256), F32),
            vmem((3 * C, 256), BF16),
            vmem((3 * F, 256), BF16),
            vmem((F, 128), F32),
            vmem((F, 128), F32),
            dma((CHUNKS,)), dma((CHUNKS,)), dma, dma, dma, dma,
            dma((CHUNKS,)), dma((CHUNKS,)), dma, dma,
            dma((CHUNKS,)), dma((CHUNKS,)), dma, dma,
            dma((CHUNKS,)), dma((CHUNKS,)), dma, dma,
            pltpu.SemaphoreType.REGULAR,
        ],
        compiler_params=pltpu.CompilerParams(collective_id=0, has_side_effects=True, vmem_limit_bytes=30 << 20),
    )(num.reshape(2 * CHAN, CHUNKS, 16, 128), num9, wsum, jnp.asarray(synth), jnp.asarray(forward), jnp.asarray(turn))

    out, depth = pl.pallas_call(
        gather_kernel,
        grid_spec=pltpu.PrefetchScalarGridSpec(
            num_scalar_prefetch=1,
            grid=(BEAMS_DEV,),
            in_specs=[
                pl.BlockSpec((256, 16, 128), lambda b, _: (0, 0, 0)),
                pl.BlockSpec((64, 8, 128), lambda b, _: (0, 0, 0)),
                pl.BlockSpec((512, 128), lambda b, _: (0, 0)),
                pl.BlockSpec((2, F // 4, F), lambda b, _: (0, b, 0)),
            ],
            out_specs=[
                pl.BlockSpec((1, PER, 256, 128), lambda b, _: (b, 0, 0, 0)),
                pl.BlockSpec((2, F // 4, F), lambda b, _: (0, b, 0)),
            ],
        ),
        out_shape=[shape((BEAMS_DEV, PER, 256, 128), F32), shape((2, F, F), F32)],
        compiler_params=pltpu.CompilerParams(vmem_limit_bytes=18 << 20),
    )(offsets, res.reshape(256, 16, 128), res9, weights, depth)
    out = out.reshape(4, PER, 128, 2, 128).transpose(0, 3, 1, 2, 4).reshape(4, 2, PER, 128 * 128)
    return out, depth


def solution(mesh):
    return jax.shard_map(
        body,
        mesh=mesh,
        in_specs=(P("sky", None, "chan", None), P("sky", None), P("sky")),
        out_specs=(P("sky", None, "chan", None), P(None, None, ("sky", "chan"))),
        check_vma=False,
    )
```
